32 devices in a mesh: groups: 2 (over x), domain: 16 (over z, y, core).
Axes of the slice: x: 2, y: 2, z: 4, core: 2. Of those that a mesh axis runs over, the one named last changes fastest.
Arguments:
- patches: bfloat16 [512, 125, 256], P(('groups', 'domain')), parts along dimension 0, may hold values from -6 to 6
- destination: int32 [512], P(('groups', 'domain')), parts along dimension 0, may hold values from 0 to 15, as said below
- cotangent: bfloat16 [1024, 4, 512], P(('groups', 'domain')), parts along dimension 0, may hold values from -16 to 16
- conv_weight: bfloat16 [256, 27, 64], replicated, may hold values from -0.21875 to 0.21875
- conv_bias: float32 [64], replicated, may hold values from -3 to 3
- head_weight: float32 [64, 4], replicated, may hold values from -0.75 to 0.75
Outputs:
- grad_conv: float32 [512, 27, 64], P(('groups', 'domain')), parts along dimension 0
- grad_bias: float32 [128], P('groups'), parts along dimension 0
- grad_head: float32 [128, 4], P('groups'), parts along dimension 0
The draws below stay inside these ranges and needn't reach their ends.
There are 2 independent parts, one for each index of `groups`. The reference program is written for one: setup_inputs(seed, part) draws one part's arguments, and reference() takes and returns one part's arrays. A program takes and returns all parts, laid end to end along the dimension named above; an argument that names none is the same for every part. Nothing has to cross between parts.
Inputs may be any that keep to these rules, and one draw needn't show every extreme that they name: `destination`: each trainer receives at most 32 patches and some trainer exactly 32; one owner sends at most 2 patch to one trainer and some pair reaches it; the patches of one trainer come from the owners as evenly as their number allows.
All inputs are finite; a program needn't handle non-finite values.
Results may differ from the reference program's by a relative error of at most 0.0029.
Values may be sent and summed in bfloat16 or wider, within the bound.
No kernel may reach another device: no remote copies, remote signals or barrier semaphores. Data moves between devices by JAX's collectives and lax.ppermute only.
A program may use at most 64 MiB of HBM per device.

```python
import jax
import jax.numpy as jnp
from jax import lax

C_IN = 256
C_OUT = 64
FIELDS = 4
TAPS = 27
PS = 4
OWN = 16
PAD = 5
CELLS = 125
FINE = 512
OWNERS = 16
PATCHES = 256
TCAP = 32


def draw_destination(key, part):
    pair_key, spread_key, owner_key, shuffle_key = jax.random.split(key, 4)
    pair_order = jax.random.permutation(pair_key, OWNERS)
    half_count = OWNERS // 2
    spread_amount = jax.random.randint(spread_key, (half_count,), 0, OWN + 1).astype(jnp.int32)
    spread_amount = spread_amount.at[0].set(OWN)
    counts = jnp.zeros((OWNERS,), jnp.int32)
    counts = counts.at[pair_order[0::2]].set(OWN + spread_amount)
    counts = counts.at[pair_order[1::2]].set(OWN - spread_amount)
    count_ends = jnp.cumsum(counts)
    tickets = jnp.arange(PATCHES, dtype=jnp.int32)
    trainer_of = jnp.sum((count_ends[None, :] <= tickets[:, None]).astype(jnp.int32), axis=1)
    owner_order = jax.random.permutation(owner_key, OWNERS).astype(jnp.int32)
    owner_of = owner_order[tickets % OWNERS]
    slot_of = tickets // OWNERS
    shuffles = jax.vmap(lambda sub_key: jax.random.permutation(sub_key, OWN))(jax.random.split(shuffle_key, OWNERS))
    row_of = owner_of * OWN + shuffles[owner_of, slot_of].astype(jnp.int32)
    return jnp.zeros((PATCHES,), jnp.int32).at[row_of].set(trainer_of.astype(jnp.int32))


def spiked(drawn, key, source, target, parts, factor):
    def block_of(axis_at):
        return (jnp.arange(drawn.shape[axis_at]) // (drawn.shape[axis_at] // parts)).reshape((-1,) + (1,) * (drawn.ndim - 1 - axis_at))

    near = jax.random.permutation(key, parts)[block_of(target)]
    far = (block_of(target) + parts // 2) % parts
    return jnp.where((block_of(source) == near) | (block_of(source) == far), factor * drawn, drawn)


def steps_of(rng, shape, pieces, least, high):
    loudness, own = 1.0, jax.random.fold_in(rng, 6)
    for position, shards_of in pieces:
        draws = jnp.exp(jax.random.uniform(jax.random.fold_in(own, position), (shards_of,), jnp.float32, least / len(pieces), high / len(pieces)))
        loudness = loudness * jnp.repeat(draws, shape[position] // shards_of).reshape([-1 if axis == position else 1 for axis in range(len(shape))])
    return loudness


def scatter_about(stream_key, dims, scale, reach, shards=(), kind=jnp.bfloat16):
    factor_of = steps_of(stream_key, dims, shards, -0.22, 0.18) if shards else 1.0
    array = jax.random.normal(stream_key, dims, jnp.float32) * scale * factor_of
    return jnp.minimum(jnp.maximum(array, -reach), reach).astype(kind)


def noise_with(rng, extent, spread, reach, cuts, heavy, kind=jnp.bfloat16):
    drawn = spread * jax.random.normal(rng, extent, jnp.float32)
    if cuts:
        drawn = drawn * steps_of(rng, extent, cuts, -0.22, 0.18)
    return jnp.clip(spiked(drawn, jax.random.fold_in(rng, 3), *heavy), -reach, reach).astype(kind)


def setup_inputs(seed: int = 0, part: int = 0) -> dict:
    keys = jax.random.split(jax.random.key(seed), 7)
    part_keys = jax.random.split(jax.random.fold_in(keys[6], part), 7)
    return {
        "patches": noise_with(part_keys[0], (PATCHES, CELLS, C_IN), 1.0, 6.0, ((0, 16),), (0, 2, 16, 2.0)),
        "destination": draw_destination(jax.random.fold_in(jax.random.fold_in(keys[6], part), 71), part),
        "cotangent": scatter_about(part_keys[2], (OWNERS * TCAP, FIELDS, FINE), 4.0, 16.0, ((0, 16),)),
        "conv_weight": scatter_about(keys[3], (C_IN, TAPS, C_OUT), (C_IN * TAPS // 8) ** -0.5, 0.21875),
        "conv_bias": scatter_about(keys[4], (C_OUT,), 0.5, 3.0, (), jnp.float32),
        "head_weight": scatter_about(keys[5], (C_OUT, FIELDS), C_OUT ** -0.5, 0.75, (), jnp.float32),
    }


def trained_rows(destination):
    trainer_ids = jnp.arange(OWNERS, dtype=jnp.int32)
    dest_hits = (destination[:, None] == trainer_ids[None, :]).astype(jnp.int32)
    rank_list = jnp.sum(jnp.cumsum(dest_hits, axis=0) * dest_hits, axis=1) - 1
    return (destination * TCAP + rank_list).astype(jnp.int32)


def tap_split(tap_index):
    return tap_index // 9, (tap_index // 3) % 3, tap_index % 3


def forward_block(block_patches, conv_weight, conv_bias):
    block_count = block_patches.shape[0]
    flat_cells = block_patches.reshape(block_count * PAD ** 3, C_IN)
    grid_side = 2 * PS + 3
    canvas = jnp.zeros((block_count, grid_side, grid_side, grid_side, C_OUT), jnp.float32)
    for tap_index in range(TAPS):
        first_tap, second_tap, third_tap = tap_split(tap_index)
        product = jnp.dot(flat_cells, conv_weight[:, tap_index, :], preferred_element_type=jnp.float32)
        product = product.reshape(block_count, PAD, PAD, PAD, C_OUT)
        canvas = canvas.at[:, first_tap:first_tap + 2 * PAD:2, second_tap:second_tap + 2 * PAD:2,
                           third_tap:third_tap + 2 * PAD:2, :].add(product)
    return canvas[:, 1:1 + 2 * PS, 1:1 + 2 * PS, 1:1 + 2 * PS, :] + conv_bias


def weight_block(block_patches, grad_low):
    block_count = block_patches.shape[0]
    flat_cells = block_patches.reshape(block_count * PAD ** 3, C_IN)
    padded_grad = jnp.pad(grad_low, ((0, 0), (1, 2), (1, 2), (1, 2), (0, 0)))
    columns = []
    for tap_index in range(TAPS):
        first_tap, second_tap, third_tap = tap_split(tap_index)
        tap_view = padded_grad[:, first_tap:first_tap + 2 * PAD:2, second_tap:second_tap + 2 * PAD:2,
                               third_tap:third_tap + 2 * PAD:2, :].reshape(block_count * PAD ** 3, C_OUT)
        columns.append(jnp.dot(flat_cells.T, tap_view, preferred_element_type=jnp.float32))
    return jnp.stack(columns, axis=1)


def reference(patches, destination, cotangent, conv_weight, conv_bias, head_weight):
    cot_rows = trained_rows(destination)
    block_total = PATCHES // OWN
    patch_blocks = patches.reshape(block_total, OWN, PAD, PAD, PAD, C_IN)
    row_blocks = cot_rows.reshape(block_total, OWN)
    head_full = head_weight.astype(jnp.float32)

    def step_block(running, inputs):
        conv_sum, bias_sum, head_sum = running
        block_patches, block_rows = inputs
        hidden = forward_block(block_patches, conv_weight, conv_bias)
        cot_fine = cotangent[block_rows].astype(jnp.float32).reshape(OWN, FIELDS, 2 * PS, 2 * PS, 2 * PS)
        cot_fine = cot_fine.transpose(0, 2, 3, 4, 1)
        sigmoid_h = jax.nn.sigmoid(hidden)
        active = hidden * sigmoid_h
        upstream = jnp.einsum("bxyzf,of->bxyzo", cot_fine, head_full, precision=lax.Precision.HIGHEST)
        grad_hidden = upstream * sigmoid_h * (1.0 + hidden * (1.0 - sigmoid_h))
        grad_low = grad_hidden.astype(jnp.bfloat16)
        conv_sum = conv_sum + weight_block(block_patches, grad_low)
        bias_sum = bias_sum + jnp.sum(grad_hidden, axis=(0, 1, 2, 3))
        head_sum = head_sum + jnp.einsum("bxyzo,bxyzf->of", active, cot_fine, precision=lax.Precision.HIGHEST)
        return (conv_sum, bias_sum, head_sum), None

    initial = (jnp.zeros((C_IN, TAPS, C_OUT), jnp.float32), jnp.zeros((C_OUT,), jnp.float32),
               jnp.zeros((C_OUT, FIELDS), jnp.float32))
    totals, unused_out = lax.scan(step_block, initial, (patch_blocks, row_blocks))
    grad_scale = (PATCHES * PS ** 3) ** -0.5
    return totals[0] * grad_scale, totals[1] * grad_scale, totals[2] * grad_scale
```

```python
import jax
import jax.numpy as jnp
import numpy as np
from jax import lax
from jax.experimental import pallas as pl
from jax.experimental.pallas import tpu as pltpu
from jax.sharding import PartitionSpec as P

C_IN = 256
C_OUT = 64
FIELDS = 4
TAPS = 27
PS = 4
PAD = 5
CELLS = PAD**3
FINE = 512
LANES = 128
BLOCKS = 14
SUM_ROWS = 16
F32 = jnp.float32
BF16 = jnp.bfloat16
HALF_TAPS = [(b * 3 + 1, b * 3 + 2) for b in range(9)]
HALF_TAPS += [(4 * 3, 7 * 3), (5 * 3, 8 * 3), (3 * 3, 6 * 3), (1 * 3, 2 * 3), (None, 0)]


def count_list(destination, owners):
    own = destination.shape[0]

    def body(dest_ref, out_ref):
        trainer = lax.broadcasted_iota(jnp.int32, (owners, LANES), 0)
        total = jnp.zeros((owners, LANES), jnp.int32)
        for n in range(own):
            total = total + (trainer == dest_ref[n]).astype(jnp.int32)
        out_ref[...] = total.reshape(owners, 1, LANES)

    return pl.pallas_call(
        body,
        in_specs=[pl.BlockSpec(memory_space=pltpu.SMEM)],
        out_specs=pl.BlockSpec(memory_space=pltpu.VMEM),
        out_shape=jax.ShapeDtypeStruct((owners, 1, LANES), jnp.int32),
        name="count_list",
    )(destination)


def row_copy(counts, rows, per_pair):
    owners = counts.shape[0]
    limit = rows.shape[0] - 1

    def body(count_ref, rows_ref, out_ref):
        def one_owner(owner, start):
            for rank in range(per_pair):
                out_ref[owner * per_pair + rank] = rows_ref[jnp.minimum(start + rank, limit)]
            return start + count_ref[owner, 0, 0]

        lax.fori_loop(0, owners, one_owner, jnp.int32(0))

    return pl.pallas_call(
        body,
        in_specs=[
            pl.BlockSpec(memory_space=pltpu.SMEM),
            pl.BlockSpec(memory_space=pltpu.VMEM),
        ],
        out_specs=pl.BlockSpec(memory_space=pltpu.VMEM),
        out_shape=jax.ShapeDtypeStruct((owners * per_pair,) + rows.shape[1:], rows.dtype),
        name="row_copy",
    )(counts, rows)


def head_terms(head):
    rows = jnp.concatenate([jnp.broadcast_to(head[f : f + 1], (32, C_OUT)) for f in range(FIELDS)], axis=0)
    pair = jnp.concatenate([rows, rows], axis=1)
    table = jnp.concatenate([pair] * 4, axis=1)
    row = lax.broadcasted_iota(jnp.int32, table.shape, 0)
    col = lax.broadcasted_iota(jnp.int32, table.shape, 1)
    table = jnp.where(row % 8 == col // C_OUT, table, 0.0)
    high = table.astype(BF16)
    return high, (table - high.astype(F32)).astype(BF16)


def forward_part(patches, first, count, weights, bias, destination, head, per_pair):
    own = patches.shape[1]
    rows = 16 * own
    lead = first == 0

    def body(*refs):
        dest_ref, head_ref, x_ref, w_ref, bias_ref = refs[:5]
        xt_ref, dact_ref, act_ref = refs[5:8]
        w2_ref = refs[-1]
        step = pl.program_id(0)

        @pl.when(step == 0)
        def _():
            w2_ref[1, :, 0:C_OUT, :] = jnp.zeros((9, C_OUT, C_IN), BF16)
            for b in range(9):
                w2_ref[0, b] = w_ref[3 * b + 1 : 3 * b + 3].reshape(2 * C_OUT, C_IN)
                w2_ref[1, b, C_OUT:, :] = w_ref[3 * b]
            if lead:
                places_ref, table_ref = refs[8:10]
                for n in range(own):
                    rank = jnp.int32(0)
                    for k in range(n):
                        rank = rank + (dest_ref[k] == dest_ref[n]).astype(jnp.int32)
                    places_ref[n] = dest_ref[n] * per_pair + rank
                table_ref[0], table_ref[1] = head_terms(head_ref[...])

        m1 = step + first
        picked = []
        for shift in range(8):
            s1, s2, s3 = shift // 4, (shift // 2) % 2, shift % 2
            pieces = [
                x_ref[pl.ds((m1 + s1) * 25 + (m2 + s2) * 5 + s3, 4)].reshape(4 * own, C_IN)
                for m2 in range(4)
            ]
            value = jnp.concatenate(pieces, axis=0)
            picked.append(value)
            xt_ref[shift] = value.T
        bias_row = jnp.concatenate([bias_ref[...]] * 4, axis=1)
        for p1 in range(2):
            both = jnp.zeros((rows, 2 * LANES), F32)
            odd = jnp.zeros((rows, LANES), F32)
            for s1 in range(p1 + 1):
                k1 = 1 if p1 == 0 else (2 if s1 == 0 else 0)
                for s3 in range(2):
                    both = both + lax.dot_general(
                        picked[s1 * 4 + s3],
                        w2_ref[s3, k1 * 3 + 1 : k1 * 3 + 3].reshape(2 * LANES, C_IN),
                        (((1,), (1,)), ((), ())),
                        preferred_element_type=F32,
                    )
                    odd = odd + lax.dot_general(
                        picked[s1 * 4 + 2 + s3],
                        w2_ref[s3, k1 * 3],
                        (((1,), (1,)), ((), ())),
                        preferred_element_type=F32,
                    )
            hidden = jnp.concatenate([both[:, :LANES], both[:, LANES:] + odd], axis=1) + bias_row
            gate = jax.nn.sigmoid(hidden)
            active = hidden * gate
            lanes = slice(p1 * 2 * LANES, (p1 + 1) * 2 * LANES)
            dact_ref[:, lanes] = gate * (1.0 + hidden * (1.0 - gate))
            high = active.astype(BF16)
            act_ref[0, :, lanes] = high
            act_ref[1, :, lanes] = (active - high.astype(F32)).astype(BF16)

    fixed = lambda *shape: pl.BlockSpec(shape, lambda i: (0,) * len(shape))
    out_specs = [
        pl.BlockSpec((8, C_IN, rows), lambda i: (0, 0, i)),
        pl.BlockSpec((rows, 512), lambda i: (i, 0)),
        pl.BlockSpec((2, rows, 512), lambda i: (0, i, 0)),
    ]
    out_shape = [
        jax.ShapeDtypeStruct((8, C_IN, count * rows), BF16),
        jax.ShapeDtypeStruct((count * rows, 512), F32),
        jax.ShapeDtypeStruct((2, count * rows, 512), BF16),
    ]
    if lead:
        out_specs += [pl.BlockSpec(memory_space=pltpu.SMEM), fixed(2, LANES, 512)]
        out_shape += [
            jax.ShapeDtypeStruct((own,), jnp.int32),
            jax.ShapeDtypeStruct((2, LANES, 512), BF16),
        ]
    return pl.pallas_call(
        body,
        grid=(count,),
        in_specs=[
            pl.BlockSpec(memory_space=pltpu.SMEM),
            fixed(FIELDS, C_OUT),
            fixed(CELLS, own, C_IN),
            fixed(TAPS, C_OUT, C_IN),
            fixed(1, C_OUT),
        ],
        out_specs=out_specs,
        out_shape=out_shape,
        scratch_shapes=[pltpu.VMEM((2, 9, LANES, C_IN), BF16)],
        cost_estimate=pl.CostEstimate(
            flops=count * 2 * rows * C_IN * 3600, transcendentals=0, bytes_accessed=4 << 20
        ),
        name="forward_part",
    )(destination, head, patches, weights, bias)


def split_sums(sums):
    high = sums.astype(BF16)
    rest = sums - high.astype(F32)
    middle = rest.astype(BF16)
    low = (rest - middle.astype(F32)).astype(BF16)
    low_lanes = lax.broadcasted_iota(jnp.int32, sums.shape, 1) < C_OUT
    first = jnp.where(low_lanes, high.astype(F32), pltpu.roll(middle.astype(F32), C_OUT, 1))
    second = jnp.where(low_lanes, low.astype(F32), 0.0)
    return jnp.concatenate([first, second], axis=0).astype(BF16)


def join_sums(rows):
    return rows[0:8] + pltpu.roll(rows[0:8], C_OUT, 1) + rows[8:16]


def backward(places, core, arrived, head_table, parts, slots):
    part_count = len(parts)
    part_rows = parts[0][1].shape[0]
    rows = part_count * part_rows
    steps = part_rows // (16 * slots)
    span = 16 * slots
    groups = C_IN // 32

    def body(*refs):
        places_ref, core_ref, arrived_ref, head_ref = refs[:4]
        sources = refs[4 : 4 + 3 * part_count]
        keep_ref, send_ref, sums_ref = refs[4 + 3 * part_count : 7 + 3 * part_count]
        xt_ref, dact_ref, act_ref, dsel_ref, grad_ref, pack_ref, sem = refs[7 + 3 * part_count :]
        copies = []
        for part in range(part_count):
            xt_hbm, dact_hbm, act_hbm = sources[3 * part : 3 * part + 3]
            copies.append(
                (
                    pltpu.make_async_copy(dact_hbm, dact_ref.at[part], sem.at[0, part]),
                    pltpu.make_async_copy(act_hbm, act_ref.at[part], sem.at[1, part]),
                    pltpu.make_async_copy(xt_hbm, xt_ref.at[part], sem.at[2, part]),
                )
            )
        for kind in range(3):
            for part in range(part_count):
                copies[part][kind].start()
        for n in range(slots):
            dsel_ref[:, n, :] = arrived_ref[places_ref[n]].astype(F32)
        fields = dsel_ref[...].reshape(span, LANES).astype(BF16)
        lane = lax.broadcasted_iota(jnp.int32, (1, LANES), 1)
        low_lanes = lane < C_OUT
        bias_sum = jnp.zeros((1, 512), F32)
        head_sum = jnp.zeros((LANES, 512), F32)
        for part in range(part_count):
            copies[part][0].wait()
            copies[part][1].wait()
            for step in range(steps):
                m1 = part * steps + step
                here = slice(step * span, (step + 1) * span)
                there = slice(m1 * span, (m1 + 1) * span)
                mine = (lane // 8) % 4 == m1
                some = jnp.where(mine, fields, jnp.zeros_like(fields))
                upstream = jnp.dot(some, head_ref[0], preferred_element_type=F32)
                upstream = upstream + jnp.dot(some, head_ref[1], preferred_element_type=F32)
                grad = upstream * dact_ref[part, here, :]
                bias_sum = bias_sum + jnp.sum(grad, axis=0, keepdims=True)
                grad_ref[there, :] = grad.astype(BF16)
                blk = [grad[:, b * LANES : (b + 1) * LANES] for b in range(4)]
                for k, (lo, hi) in enumerate(((0, 2), (1, 3), (2, 3))):
                    packed = jnp.where(low_lanes, pltpu.roll(blk[lo], C_OUT, 1), blk[hi])
                    pack_ref[there, k * LANES : (k + 1) * LANES] = packed.astype(BF16)
                for term in range(2):
                    head_sum = head_sum + lax.dot_general(
                        some,
                        act_ref[part, term, here, :],
                        (((0,), (0,)), ((), ())),
                        preferred_element_type=F32,
                    )
        row = lax.broadcasted_iota(jnp.int32, (LANES, 512), 0)
        col = lax.broadcasted_iota(jnp.int32, (LANES, 512), 1)
        head_sum = jnp.where(row % 8 == col // C_OUT, head_sum, 0.0)
        heads = [
            jnp.sum(head_sum[f * 32 : (f + 1) * 32], axis=0, keepdims=True) for f in range(FIELDS)
        ]
        stacked = jnp.concatenate([bias_sum] + heads + [jnp.zeros((3, 512), F32)], axis=0)
        folded = sum(stacked[:, b * LANES : (b + 1) * LANES] for b in range(4))
        folded = folded + pltpu.roll(folded, C_OUT, 1)
        sums_ref[...] = folded
        send_ref[groups * BLOCKS * 16 :, :] = split_sums(folded)
        mine_core = core_ref[0]
        for part in range(part_count):
            copies[part][2].wait()

        def product(shift, at_ref, lanes):
            result = None
            for part in range(part_count):
                term = jnp.dot(
                    xt_ref[part, shift],
                    at_ref[part * part_rows : (part + 1) * part_rows, lanes],
                    preferred_element_type=F32,
                )
                result = term if result is None else result + term
            return result

        def put(block, value):
            split = value.reshape(groups, 2, 16, LANES)
            even, odd = split[:, 0], split[:, 1]
            keep_ref[:, block * 16 : (block + 1) * 16, :] = jnp.where(mine_core == 0, even, odd)
            other = jnp.where(mine_core == 0, odd, even).astype(BF16)
            for g in range(groups):
                send_ref[(g * BLOCKS + block) * 16 : (g * BLOCKS + block + 1) * 16, :] = other[g]

        for shift, lo, count, blocks in (
            (0, 0, 2, (4, 5)),
            (0, 2, 2, (7, 8)),
            (4, 2, 2, (1, 2)),
            (6, 3, 1, (0,)),
        ):
            value = product(shift, grad_ref, slice(lo * LANES, (lo + count) * LANES))
            for k, block in enumerate(blocks):
                put(block, value[:, k * LANES : (k + 1) * LANES])
        put(3, product(2, grad_ref, slice(LANES, 2 * LANES)))
        put(6, product(2, grad_ref, slice(3 * LANES, 4 * LANES)))
        value = product(1, pack_ref, slice(0, 2 * LANES))
        put(9, value[:, 0:LANES])
        put(10, value[:, LANES:])
        put(11, product(3, pack_ref, slice(LANES, 2 * LANES)))
        put(12, product(5, pack_ref, slice(2 * LANES, 3 * LANES)))
        put(13, product(7, pack_ref, slice(LANES, 2 * LANES)))

    smem = pl.BlockSpec(memory_space=pltpu.SMEM)
    vmem = pl.BlockSpec(memory_space=pltpu.VMEM)
    hbm = pl.BlockSpec(memory_space=pl.ANY)
    return pl.pallas_call(
        body,
        in_specs=[smem, smem, vmem, vmem] + [hbm] * (3 * part_count),
        out_specs=[vmem, vmem, vmem],
        out_shape=[
            jax.ShapeDtypeStruct((groups, BLOCKS * 16, LANES), F32),
            jax.ShapeDtypeStruct((groups * BLOCKS * 16 + SUM_ROWS, LANES), BF16),
            jax.ShapeDtypeStruct((8, LANES), F32),
        ],
        scratch_shapes=[
            pltpu.VMEM((part_count, 8, C_IN, part_rows), BF16),
            pltpu.VMEM((part_count, part_rows, 512), F32),
            pltpu.VMEM((part_count, 2, part_rows, 512), BF16),
            pltpu.VMEM((16, slots, LANES), F32),
            pltpu.VMEM((rows, 512), BF16),
            pltpu.VMEM((rows, 3 * LANES), BF16),
            pltpu.SemaphoreType.DMA((3, part_count)),
        ],
        name="backward",
    )(places, core, arrived, head_table, *[a for part in parts for a in part])


def pair_sum(keep, sums, other):
    groups, block_rows, _ = keep.shape

    def body(keep_ref, sums_ref, other_ref, out_ref):
        theirs = join_sums(other_ref[groups * block_rows :, :].astype(F32))
        tail = split_sums(sums_ref[...] + theirs)
        for g in range(groups):
            partner = other_ref[g * block_rows : (g + 1) * block_rows, :].astype(F32)
            out_ref[g, 0:block_rows, :] = (keep_ref[g] + partner).astype(BF16)
            out_ref[g, block_rows:, :] = tail

    return pl.pallas_call(
        body,
        out_shape=jax.ShapeDtypeStruct((groups, block_rows + SUM_ROWS, LANES), BF16),
        name="pair_sum",
    )(keep, sums, other)


def final_sum(arrived, scale, per_block):
    sources, all_rows, _ = arrived.shape
    block_rows = all_rows - SUM_ROWS

    def body(in_ref, conv_ref, bias_ref, head_ref):
        total = in_ref[0].astype(F32)
        for source in range(1, sources):
            total = total + in_ref[source].astype(F32)
        total = total * scale
        for block, taps in enumerate(HALF_TAPS):
            for half, tap in enumerate(taps):
                if tap is not None:
                    conv_ref[tap] = total[
                        block * per_block : (block + 1) * per_block, half * C_OUT : (half + 1) * C_OUT
                    ]
        joined = join_sums(total[block_rows:])
        bias_ref[...] = joined[0:1, 0:C_OUT]
        head_ref[...] = joined[1 : 1 + FIELDS, 0:C_OUT]

    return pl.pallas_call(
        body,
        out_shape=[
            jax.ShapeDtypeStruct((TAPS, per_block, C_OUT), F32),
            jax.ShapeDtypeStruct((1, C_OUT), F32),
            jax.ShapeDtypeStruct((FIELDS, C_OUT), F32),
        ],
        name="final_sum",
    )(arrived)


def on_device(patches, destination, cotangent, conv_weight, conv_bias, head_weight):
    owners = lax.axis_size("domain")
    my_index = lax.axis_index("domain")
    own_rows = patches.shape[0]
    train_rows = cotangent.shape[0]
    per_pair = (train_rows + owners - 1) // owners
    channels = C_IN // owners
    splits = 16 // channels
    if splits > 1:
        order = np.arange(C_IN).reshape(C_IN // 32, splits, 2, channels)
        order = order.transpose(0, 2, 1, 3).reshape(-1)
        patches = patches[:, :, order]
        conv_weight = conv_weight[order]

    counts = lax.all_to_all(
        count_list(destination, owners), "domain", split_axis=0, concat_axis=0, tiled=True
    )

    rows = cotangent.reshape(train_rows, FIELDS, 4, 2, 4, 2, 4, 2)
    rows = rows.transpose(0, 4, 6, 1, 2, 3, 5, 7).reshape(train_rows, 16, LANES)
    outgoing = row_copy(counts, rows, per_pair)
    arrived = lax.all_to_all(
        outgoing.reshape(owners, per_pair, 16, LANES), "domain", split_axis=0, concat_axis=0, tiled=True
    ).reshape(owners * per_pair, 16, LANES)

    cells = patches.transpose(1, 0, 2)
    weights = conv_weight.transpose(1, 2, 0)
    parts = [
        forward_part(
            cells, first, 2, weights, conv_bias.reshape(1, C_OUT), destination, head_weight.T, per_pair
        )
        for first in (0, 2)
    ]
    places, head_table = parts[0][3:]
    parts = [part[:3] for part in parts]
    core = (my_index % 2).astype(jnp.int32).reshape(1)
    keep, send, sums = backward(places, core, arrived, head_table, parts, own_rows)
    other = lax.ppermute(send, "domain", [(i, i ^ 1) for i in range(owners)])
    payload = pair_sum(keep, sums, other)

    scale = float((owners * own_rows * PS**3) ** (-0.5))
    mates = owners // 2
    groups = [[core_id + 2 * k for k in range(mates)] for core_id in range(2)]
    block_rows = BLOCKS * 16
    if splits > 1:
        tail = jnp.repeat(payload[:, block_rows:], splits, axis=0)
        blocks = payload[:, :block_rows].reshape(C_IN // 32, BLOCKS, splits, channels, LANES)
        blocks = blocks.transpose(0, 2, 1, 3, 4).reshape(mates, BLOCKS * channels, LANES)
        payload = jnp.concatenate([blocks, tail], axis=1)
    swapped = lax.all_to_all(
        payload, "domain", split_axis=0, concat_axis=0, tiled=True, axis_index_groups=groups
    )
    if splits > 1:
        tail = jnp.sum(swapped[:, BLOCKS * channels :].astype(F32), axis=0) * scale
        tail = tail[0:8, 0:C_OUT] + tail[0:8, C_OUT:] + tail[8:, 0:C_OUT]
        total = jnp.sum(swapped[:, : BLOCKS * channels].astype(F32), axis=0) * scale
        total = total.reshape(BLOCKS, channels, 2, C_OUT)
        where = {tap: (b, h) for b, pair in enumerate(HALF_TAPS) for h, tap in enumerate(pair)}
        conv = jnp.stack([total[where[t][0], :, where[t][1]] for t in range(TAPS)], axis=1)
        return conv, tail[0], tail[1 : 1 + FIELDS].T
    conv, bias_out, head_out = final_sum(swapped, scale, channels)
    return conv.transpose(1, 0, 2), bias_out.reshape(C_OUT), head_out.T


def solution(mesh):
    placed = (
        P(("groups", "domain"), None, None),
        P(("groups", "domain")),
        P(("groups", "domain"), None, None),
        P(),
        P(),
        P(),
    )
    return jax.shard_map(
        on_device,
        mesh=mesh,
        in_specs=placed,
        out_specs=(P(("groups", "domain"), None, None), P("groups"), P("groups", None)),
        check_vma=False,
    )
```

```python
import jax
import jax.numpy as jnp
import numpy as np
from jax import lax
from jax.experimental import pallas as pl
from jax.experimental.pallas import tpu as pltpu
from jax.sharding import PartitionSpec as P

C_IN = 256
C_OUT = 64
FIELDS = 4
TAPS = 27
PS = 4
PAD = 5
CELLS = PAD**3
FINE = 512
LANES = 128
BLOCKS = 14
SUM_ROWS = 16
F32 = jnp.float32
BF16 = jnp.bfloat16
HALF_TAPS = [(b * 3 + 1, b * 3 + 2) for b in range(9)]
HALF_TAPS += [(4 * 3, 7 * 3), (5 * 3, 8 * 3), (3 * 3, 6 * 3), (1 * 3, 2 * 3), (None, 0)]


def count_list(destination, owners):
    own = destination.shape[0]

    def body(dest_ref, out_ref):
        trainer = lax.broadcasted_iota(jnp.int32, (owners, LANES), 0)
        total = jnp.zeros((owners, LANES), jnp.int32)
        for n in range(own):
            total = total + (trainer == dest_ref[n]).astype(jnp.int32)
        out_ref[...] = total.reshape(owners, 1, LANES)

    return pl.pallas_call(
        body,
        in_specs=[pl.BlockSpec(memory_space=pltpu.SMEM)],
        out_specs=pl.BlockSpec(memory_space=pltpu.VMEM),
        out_shape=jax.ShapeDtypeStruct((owners, 1, LANES), jnp.int32),
        compiler_params=pltpu.CompilerParams(vmem_limit_bytes=1 << 20),
        name="count_list",
    )(destination)


def row_copy(counts, rows, per_pair):
    owners = counts.shape[0]
    limit = rows.shape[0] - 1

    def body(count_ref, rows_ref, out_ref):
        def one_owner(owner, start):
            for rank in range(per_pair):
                out_ref[owner * per_pair + rank] = rows_ref[jnp.minimum(start + rank, limit)]
            return start + count_ref[owner, 0, 0]

        lax.fori_loop(0, owners, one_owner, jnp.int32(0))

    return pl.pallas_call(
        body,
        in_specs=[
            pl.BlockSpec(memory_space=pltpu.SMEM),
            pl.BlockSpec(memory_space=pltpu.VMEM),
        ],
        out_specs=pl.BlockSpec(memory_space=pltpu.VMEM),
        out_shape=jax.ShapeDtypeStruct((owners * per_pair,) + rows.shape[1:], rows.dtype),
        compiler_params=pltpu.CompilerParams(vmem_limit_bytes=4 << 20),
        name="row_copy",
    )(counts, rows)


def head_terms(head):
    rows = jnp.concatenate([jnp.broadcast_to(head[f : f + 1], (32, C_OUT)) for f in range(FIELDS)], axis=0)
    pair = jnp.concatenate([rows, rows], axis=1)
    table = jnp.concatenate([pair] * 4, axis=1)
    row = lax.broadcasted_iota(jnp.int32, table.shape, 0)
    col = lax.broadcasted_iota(jnp.int32, table.shape, 1)
    table = jnp.where(row % 8 == col // C_OUT, table, 0.0)
    high = table.astype(BF16)
    return high, (table - high.astype(F32)).astype(BF16)


def forward_part(patches, first, count, weights, bias, destination, head, per_pair):
    own = patches.shape[1]
    rows = 16 * own
    lead = first == 0

    def body(*refs):
        dest_ref, head_ref, x_ref, w_ref, bias_ref = refs[:5]
        hidden_ref = refs[5]
        w2_ref = refs[-1]
        step = pl.program_id(0)

        @pl.when(step == 0)
        def _():
            w2_ref[1, :, 0:C_OUT, :] = jnp.zeros((9, C_OUT, C_IN), BF16)
            for b in range(9):
                w2_ref[0, b] = w_ref[3 * b + 1 : 3 * b + 3].reshape(2 * C_OUT, C_IN)
                w2_ref[1, b, C_OUT:, :] = w_ref[3 * b]
            if lead:
                places_ref, table_ref = refs[6:8]
                for n in range(own):
                    rank = jnp.int32(0)
                    for k in range(n):
                        rank = rank + (dest_ref[k] == dest_ref[n]).astype(jnp.int32)
                    places_ref[n] = dest_ref[n] * per_pair + rank
                table_ref[0], table_ref[1] = head_terms(head_ref[...])

        m1 = step + first
        picked = []
        for shift in range(8):
            s1, s2, s3 = shift // 4, (shift // 2) % 2, shift % 2
            pieces = [
                x_ref[pl.ds((m1 + s1) * 25 + (m2 + s2) * 5 + s3, 4)].reshape(4 * own, C_IN)
                for m2 in range(4)
            ]
            picked.append(jnp.concatenate(pieces, axis=0))
        bias_row = jnp.concatenate([bias_ref[...]] * 4, axis=1)
        for p1 in range(2):
            both = jnp.zeros((rows, 2 * LANES), F32)
            odd = jnp.zeros((rows, LANES), F32)
            for s1 in range(p1 + 1):
                k1 = 1 if p1 == 0 else (2 if s1 == 0 else 0)
                for s3 in range(2):
                    both = both + lax.dot_general(
                        picked[s1 * 4 + s3],
                        w2_ref[s3, k1 * 3 + 1 : k1 * 3 + 3].reshape(2 * LANES, C_IN),
                        (((1,), (1,)), ((), ())),
                        preferred_element_type=F32,
                    )
                    odd = odd + lax.dot_general(
                        picked[s1 * 4 + 2 + s3],
                        w2_ref[s3, k1 * 3],
                        (((1,), (1,)), ((), ())),
                        preferred_element_type=F32,
                    )
            lanes = slice(p1 * 2 * LANES, (p1 + 1) * 2 * LANES)
            total = jnp.concatenate([both[:, :LANES], both[:, LANES:] + odd], axis=1)
            hidden_ref[:, lanes] = total + bias_row

    fixed = lambda *shape: pl.BlockSpec(shape, lambda i: (0,) * len(shape))
    out_specs = [pl.BlockSpec((rows, 512), lambda i: (i, 0))]
    out_shape = [jax.ShapeDtypeStruct((count * rows, 512), F32)]
    if lead:
        out_specs += [pl.BlockSpec(memory_space=pltpu.SMEM), fixed(2, LANES, 512)]
        out_shape += [
            jax.ShapeDtypeStruct((own,), jnp.int32),
            jax.ShapeDtypeStruct((2, LANES, 512), BF16),
        ]
    return pl.pallas_call(
        body,
        grid=(count,),
        in_specs=[
            pl.BlockSpec(memory_space=pltpu.SMEM),
            fixed(FIELDS, C_OUT),
            fixed(CELLS, own, C_IN),
            fixed(TAPS, C_OUT, C_IN),
            fixed(1, C_OUT),
        ],
        out_specs=out_specs,
        out_shape=out_shape,
        scratch_shapes=[pltpu.VMEM((2, 9, LANES, C_IN), BF16)],
        cost_estimate=pl.CostEstimate(
            flops=count * 2 * rows * C_IN * 3600, transcendentals=0, bytes_accessed=4 << 20
        ),
        compiler_params=pltpu.CompilerParams(vmem_limit_bytes=16 << 20),
        name="forward_part",
    )(destination, head, patches, weights, bias)


def split_sums(sums):
    high = sums.astype(BF16)
    rest = sums - high.astype(F32)
    middle = rest.astype(BF16)
    low = (rest - middle.astype(F32)).astype(BF16)
    low_lanes = lax.broadcasted_iota(jnp.int32, sums.shape, 1) < C_OUT
    first = jnp.where(low_lanes, high.astype(F32), pltpu.roll(middle.astype(F32), C_OUT, 1))
    second = jnp.where(low_lanes, low.astype(F32), 0.0)
    return jnp.concatenate([first, second], axis=0).astype(BF16)


def join_sums(rows):
    return rows[0:8] + pltpu.roll(rows[0:8], C_OUT, 1) + rows[8:16]


def backward(places, core, arrived, head_table, cells, hiddens):
    slots = cells.shape[1]
    span = 16 * slots
    rows = 4 * span
    groups = C_IN // 32
    steps = 4 // len(hiddens)

    def body(places_ref, core_ref, arrived_ref, head_ref, x_ref, *refs):
        hidden_refs = refs[: len(hiddens)]
        keep_ref, send_ref, sums_ref, dsel_ref, grad_ref, pack_ref = refs[len(hiddens) :]
        for n in range(slots):
            dsel_ref[:, n, :] = arrived_ref[places_ref[n]].astype(F32)
        fields = dsel_ref[...].reshape(span, LANES).astype(BF16)
        lane = lax.broadcasted_iota(jnp.int32, (1, LANES), 1)
        low_lanes = lane < C_OUT
        bias_sum = jnp.zeros((1, 512), F32)
        head_sum = jnp.zeros((LANES, 512), F32)
        for m1 in range(4):
            here = slice(m1 * span, (m1 + 1) * span)
            mine = (lane // 8) % 4 == m1
            some = jnp.where(mine, fields, jnp.zeros_like(fields))
            upstream = jnp.dot(some, head_ref[0], preferred_element_type=F32)
            upstream = upstream + jnp.dot(some, head_ref[1], preferred_element_type=F32)
            hidden = hidden_refs[m1 // steps][(m1 % steps) * span : (m1 % steps + 1) * span, :]
            gate = jax.nn.sigmoid(hidden)
            active = hidden * gate
            grad = upstream * (gate * (1.0 + hidden * (1.0 - gate)))
            bias_sum = bias_sum + jnp.sum(grad, axis=0, keepdims=True)
            grad_ref[here, :] = grad.astype(BF16)
            blk = [grad[:, b * LANES : (b + 1) * LANES] for b in range(4)]
            for k, (lo, hi) in enumerate(((0, 2), (1, 3), (2, 3))):
                packed = jnp.where(low_lanes, pltpu.roll(blk[lo], C_OUT, 1), blk[hi])
                pack_ref[here, k * LANES : (k + 1) * LANES] = packed.astype(BF16)
            high = active.astype(BF16)
            for term in (high, (active - high.astype(F32)).astype(BF16)):
                head_sum = head_sum + lax.dot_general(
                    some, term, (((0,), (0,)), ((), ())), preferred_element_type=F32
                )
        row = lax.broadcasted_iota(jnp.int32, (LANES, 512), 0)
        col = lax.broadcasted_iota(jnp.int32, (LANES, 512), 1)
        head_sum = jnp.where(row % 8 == col // C_OUT, head_sum, 0.0)
        heads = [
            jnp.sum(head_sum[f * 32 : (f + 1) * 32], axis=0, keepdims=True) for f in range(FIELDS)
        ]
        stacked = jnp.concatenate([bias_sum] + heads + [jnp.zeros((3, 512), F32)], axis=0)
        folded = sum(stacked[:, b * LANES : (b + 1) * LANES] for b in range(4))
        folded = folded + pltpu.roll(folded, C_OUT, 1)
        sums_ref[...] = folded
        send_ref[groups * BLOCKS * 16 :, :] = split_sums(folded)
        mine_core = core_ref[0]

        def product(shift, at_ref, lanes):
            s1, s2, s3 = shift // 4, (shift // 2) % 2, shift % 2
            pieces = []
            for m in range(16):
                cell = (m // 4 + s1) * 25 + (m % 4 + s2) * 5 + s3
                pieces.append(x_ref[cell : cell + 4].reshape(4 * slots, C_IN))
            return lax.dot_general(
                jnp.concatenate(pieces, axis=0),
                at_ref[:, lanes],
                (((0,), (0,)), ((), ())),
                preferred_element_type=F32,
            )

        def put(block, value):
            split = value.reshape(groups, 2, 16, LANES)
            even, odd = split[:, 0], split[:, 1]
            keep_ref[:, block * 16 : (block + 1) * 16, :] = jnp.where(mine_core == 0, even, odd)
            other = jnp.where(mine_core == 0, odd, even).astype(BF16)
            for g in range(groups):
                send_ref[(g * BLOCKS + block) * 16 : (g * BLOCKS + block + 1) * 16, :] = other[g]

        value = product(0, grad_ref, slice(0, 4 * LANES))
        for k, block in enumerate((4, 5, 7, 8)):
            put(block, value[:, k * LANES : (k + 1) * LANES])
        value = product(4, grad_ref, slice(2 * LANES, 4 * LANES))
        put(1, value[:, 0:LANES])
        put(2, value[:, LANES:])
        put(0, product(6, grad_ref, slice(3 * LANES, 4 * LANES)))
        value = product(2, grad_ref, slice(LANES, 4 * LANES))
        put(3, value[:, 0:LANES])
        put(6, value[:, 2 * LANES :])
        value = product(1, pack_ref, slice(0, 2 * LANES))
        put(9, value[:, 0:LANES])
        put(10, value[:, LANES:])
        put(11, product(3, pack_ref, slice(LANES, 2 * LANES)))
        put(12, product(5, pack_ref, slice(2 * LANES, 3 * LANES)))
        put(13, product(7, pack_ref, slice(LANES, 2 * LANES)))

    smem = pl.BlockSpec(memory_space=pltpu.SMEM)
    vmem = pl.BlockSpec(memory_space=pltpu.VMEM)
    return pl.pallas_call(
        body,
        in_specs=[smem, smem] + [vmem] * (3 + len(hiddens)),
        out_specs=[vmem, vmem, vmem],
        out_shape=[
            jax.ShapeDtypeStruct((groups, BLOCKS * 16, LANES), F32),
            jax.ShapeDtypeStruct((groups * BLOCKS * 16 + SUM_ROWS, LANES), BF16),
            jax.ShapeDtypeStruct((8, LANES), F32),
        ],
        scratch_shapes=[
            pltpu.VMEM((16, slots, LANES), F32),
            pltpu.VMEM((rows, 512), BF16),
            pltpu.VMEM((rows, 3 * LANES), BF16),
        ],
        compiler_params=pltpu.CompilerParams(vmem_limit_bytes=24 << 20),
        name="backward",
    )(places, core, arrived, head_table, cells, *hiddens)


def pair_sum(keep, sums, other):
    groups, block_rows, _ = keep.shape

    def body(keep_ref, sums_ref, other_ref, out_ref):
        theirs = join_sums(other_ref[groups * block_rows :, :].astype(F32))
        tail = split_sums(sums_ref[...] + theirs)
        for g in range(groups):
            partner = other_ref[g * block_rows : (g + 1) * block_rows, :].astype(F32)
            out_ref[g, 0:block_rows, :] = (keep_ref[g] + partner).astype(BF16)
            out_ref[g, block_rows:, :] = tail

    return pl.pallas_call(
        body,
        out_shape=jax.ShapeDtypeStruct((groups, block_rows + SUM_ROWS, LANES), BF16),
        compiler_params=pltpu.CompilerParams(vmem_limit_bytes=8 << 20),
        name="pair_sum",
    )(keep, sums, other)


def final_sum(arrived, scale, per_block):
    sources, all_rows, _ = arrived.shape
    block_rows = all_rows - SUM_ROWS

    def body(in_ref, conv_ref, bias_ref, head_ref):
        total = in_ref[0].astype(F32)
        for source in range(1, sources):
            total = total + in_ref[source].astype(F32)
        total = total * scale
        for block, taps in enumerate(HALF_TAPS):
            for half, tap in enumerate(taps):
                if tap is not None:
                    conv_ref[tap] = total[
                        block * per_block : (block + 1) * per_block, half * C_OUT : (half + 1) * C_OUT
                    ]
        joined = join_sums(total[block_rows:])
        bias_ref[...] = joined[0:1, 0:C_OUT]
        head_ref[...] = joined[1 : 1 + FIELDS, 0:C_OUT]

    return pl.pallas_call(
        body,
        out_shape=[
            jax.ShapeDtypeStruct((TAPS, per_block, C_OUT), F32),
            jax.ShapeDtypeStruct((1, C_OUT), F32),
            jax.ShapeDtypeStruct((FIELDS, C_OUT), F32),
        ],
        compiler_params=pltpu.CompilerParams(vmem_limit_bytes=4 << 20),
        name="final_sum",
    )(arrived)


def on_device(patches, destination, cotangent, conv_weight, conv_bias, head_weight):
    owners = lax.axis_size("domain")
    my_index = lax.axis_index("domain")
    own_rows = patches.shape[0]
    train_rows = cotangent.shape[0]
    per_pair = (train_rows + owners - 1) // owners
    channels = C_IN // owners
    splits = 16 // channels
    if splits > 1:
        order = np.arange(C_IN).reshape(C_IN // 32, splits, 2, channels)
        order = order.transpose(0, 2, 1, 3).reshape(-1)
        patches = patches[:, :, order]
        conv_weight = conv_weight[order]

    counts = lax.all_to_all(
        count_list(destination, owners), "domain", split_axis=0, concat_axis=0, tiled=True
    )

    rows = cotangent.reshape(train_rows, FIELDS, 4, 2, 4, 2, 4, 2)
    rows = rows.transpose(0, 4, 6, 1, 2, 3, 5, 7).reshape(train_rows, 16, LANES)
    outgoing = row_copy(counts, rows, per_pair)
    arrived = lax.all_to_all(
        outgoing.reshape(owners, per_pair, 16, LANES), "domain", split_axis=0, concat_axis=0, tiled=True
    ).reshape(owners * per_pair, 16, LANES)

    cells = patches.transpose(1, 0, 2)
    weights = conv_weight.transpose(1, 2, 0)
    parts = [
        forward_part(
            cells, first, 2, weights, conv_bias.reshape(1, C_OUT), destination, head_weight.T, per_pair
        )
        for first in (0, 2)
    ]
    places, head_table = parts[0][1:]
    core = (my_index % 2).astype(jnp.int32).reshape(1)
    keep, send, sums = backward(
        places, core, arrived, head_table, cells, [part[0] for part in parts]
    )
    other = lax.ppermute(send, "domain", [(i, i ^ 1) for i in range(owners)])
    payload = pair_sum(keep, sums, other)

    scale = float((owners * own_rows * PS**3) ** (-0.5))
    mates = owners // 2
    groups = [[core_id + 2 * k for k in range(mates)] for core_id in range(2)]
    block_rows = BLOCKS * 16
    if splits > 1:
        tail = jnp.repeat(payload[:, block_rows:], splits, axis=0)
        blocks = payload[:, :block_rows].reshape(C_IN // 32, BLOCKS, splits, channels, LANES)
        blocks = blocks.transpose(0, 2, 1, 3, 4).reshape(mates, BLOCKS * channels, LANES)
        payload = jnp.concatenate([blocks, tail], axis=1)
    swapped = lax.all_to_all(
        payload, "domain", split_axis=0, concat_axis=0, tiled=True, axis_index_groups=groups
    )
    if splits > 1:
        tail = jnp.sum(swapped[:, BLOCKS * channels :].astype(F32), axis=0) * scale
        tail = tail[0:8, 0:C_OUT] + tail[0:8, C_OUT:] + tail[8:, 0:C_OUT]
        total = jnp.sum(swapped[:, : BLOCKS * channels].astype(F32), axis=0) * scale
        total = total.reshape(BLOCKS, channels, 2, C_OUT)
        where = {tap: (b, h) for b, pair in enumerate(HALF_TAPS) for h, tap in enumerate(pair)}
        conv = jnp.stack([total[where[t][0], :, where[t][1]] for t in range(TAPS)], axis=1)
        return conv, tail[0], tail[1 : 1 + FIELDS].T
    conv, bias_out, head_out = final_sum(swapped, scale, channels)
    return conv.transpose(1, 0, 2), bias_out.reshape(C_OUT), head_out.T


def solution(mesh):
    placed = (
        P(("groups", "domain"), None, None),
        P(("groups", "domain")),
        P(("groups", "domain"), None, None),
        P(),
        P(),
        P(),
    )
    return jax.shard_map(
        on_device,
        mesh=mesh,
        in_specs=placed,
        out_specs=(P(("groups", "domain"), None, None), P("groups"), P("groups", None)),
        check_vma=False,
    )
```

```python
import jax
import jax.numpy as jnp
import numpy as np
from jax import lax
from jax.experimental import pallas as pl
from jax.experimental.pallas import tpu as pltpu
from jax.sharding import PartitionSpec as P

C_IN = 256
C_OUT = 64
FIELDS = 4
TAPS = 27
PS = 4
PAD = 5
CELLS = PAD**3
FINE = 512
LANES = 128
BLOCKS = 14
F32 = jnp.float32
BF16 = jnp.bfloat16
HALF_TAPS = [(b * 3 + 1, b * 3 + 2) for b in range(9)]
HALF_TAPS += [(4 * 3, 7 * 3), (5 * 3, 8 * 3), (3 * 3, 6 * 3), (1 * 3, 2 * 3), (None, 0)]


def row_copy(listing, me, rows, per_pair):
    owners, _, own = listing.shape
    lines = owners * per_pair * FIELDS

    def body(me_ref, listing_ref, rows_ref, out_ref):
        hits = (listing_ref[...].reshape(owners, own) == me_ref[0]).astype(F32)
        counts = jnp.broadcast_to(jnp.sum(hits, axis=1, keepdims=True), (owners, LANES)).astype(BF16)
        line = lax.broadcasted_iota(jnp.int32, (lines, owners), 0)
        owner = lax.broadcasted_iota(jnp.int32, (lines, owners), 1)
        before = (owner < line // (per_pair * FIELDS)).astype(F32).astype(BF16)
        starts = jnp.dot(before, counts, preferred_element_type=F32)
        line = lax.broadcasted_iota(jnp.int32, (lines, LANES), 0)
        lane = lax.broadcasted_iota(jnp.int32, (lines, LANES), 1)
        wanted = starts.astype(jnp.int32) * FIELDS + line % (per_pair * FIELDS)
        pick = (wanted == lane).astype(F32).astype(BF16)
        out_ref[...] = jnp.dot(pick, rows_ref[...], preferred_element_type=F32).astype(BF16)

    vmem = pl.BlockSpec(memory_space=pltpu.VMEM)
    return pl.pallas_call(
        body,
        in_specs=[pl.BlockSpec(memory_space=pltpu.SMEM), vmem, vmem],
        out_specs=vmem,
        out_shape=jax.ShapeDtypeStruct((lines, FINE), BF16),
        compiler_params=pltpu.CompilerParams(vmem_limit_bytes=4 << 20),
        cost_estimate=pl.CostEstimate(flops=8 << 30, transcendentals=0, bytes_accessed=1 << 20),
        name="row_copy",
    )(me, listing, rows)


def spread(destination, owners):
    own = destination.shape[0]

    def body(in_ref, out_ref):
        out_ref[...] = jnp.broadcast_to(in_ref[...].reshape(1, 1, own), (owners, 1, own))

    return pl.pallas_call(
        body, out_shape=jax.ShapeDtypeStruct((owners, 1, own), jnp.int32), name="spread"
    )(destination.reshape(1, own))


def turn_terms():
    fine = lax.broadcasted_iota(jnp.int32, (LANES, LANES), 0)
    lane = lax.broadcasted_iota(jnp.int32, (LANES, LANES), 1)
    to = ((fine >> 4) & 3) * 32 + (fine >> 6) * 16 + (fine & 15)
    return (to == lane).astype(F32).astype(BF16)


def head_terms(head):
    rows = jnp.concatenate([jnp.broadcast_to(head[f : f + 1], (32, C_OUT)) for f in range(FIELDS)], axis=0)
    pair = jnp.concatenate([rows, rows], axis=1)
    table = jnp.concatenate([pair] * 4, axis=1)
    row = lax.broadcasted_iota(jnp.int32, table.shape, 0)
    col = lax.broadcasted_iota(jnp.int32, table.shape, 1)
    table = jnp.where((row // 8 % 4) * 2 + row % 2 == col // C_OUT, table, 0.0)
    high = table.astype(BF16)
    return jnp.concatenate([high, (table - high.astype(F32)).astype(BF16)], axis=0)


def forward_part(patches, first, count, weights, bias, destination, head, slots, per_pair):
    own = patches.shape[1]
    rows = 16 * own
    lead = first == 0

    def body(*refs):
        dest_ref, head_ref, x_ref, w_ref, bias_ref = refs[:5]
        hidden_ref = refs[5]
        w2_ref = refs[-1]
        step = pl.program_id(0)

        @pl.when(step == 0)
        def _():
            w2_ref[1, :, 0:C_OUT, :] = jnp.zeros((9, C_OUT, C_IN), BF16)
            for b in range(9):
                w2_ref[0, b] = w_ref[3 * b + 1 : 3 * b + 3].reshape(2 * C_OUT, C_IN)
                w2_ref[1, b, C_OUT:, :] = w_ref[3 * b]
            if lead:
                pick_ref, table_ref = refs[6:8]
                line = lax.broadcasted_iota(jnp.int32, (FIELDS * own, slots * FIELDS), 0)
                lane = lax.broadcasted_iota(jnp.int32, (FIELDS * own, slots * FIELDS), 1)
                wanted = jnp.zeros_like(line)
                for n in range(own):
                    rank = jnp.int32(0)
                    for k in range(n):
                        rank = rank + (dest_ref[k] == dest_ref[n]).astype(jnp.int32)
                    wanted = jnp.where(line % own == n, dest_ref[n] * per_pair + rank, wanted)
                wanted = wanted * FIELDS + line // own
                pick_ref[...] = (wanted == lane).astype(F32).astype(BF16)
                table_ref[...] = head_terms(head_ref[...])

        m1 = step + first
        picked = []
        for shift in range(8):
            s1, s2, s3 = shift // 4, (shift // 2) % 2, shift % 2
            pieces = [
                x_ref[pl.ds((m1 + s1) * 25 + (m2 + s2) * 5 + s3, 4)].reshape(4 * own, C_IN)
                for m2 in range(4)
            ]
            picked.append(jnp.concatenate(pieces, axis=0))
        bias_row = jnp.concatenate([bias_ref[...]] * 4, axis=1)
        for p1 in range(2):
            both = jnp.zeros((rows, 2 * LANES), F32)
            odd = jnp.zeros((rows, LANES), F32)
            for s1 in range(p1 + 1):
                k1 = 1 if p1 == 0 else (2 if s1 == 0 else 0)
                for s3 in range(2):
                    both = both + lax.dot_general(
                        picked[s1 * 4 + s3],
                        w2_ref[s3, k1 * 3 + 1 : k1 * 3 + 3].reshape(2 * LANES, C_IN),
                        (((1,), (1,)), ((), ())),
                        preferred_element_type=F32,
                    )
                    odd = odd + lax.dot_general(
                        picked[s1 * 4 + 2 + s3],
                        w2_ref[s3, k1 * 3],
                        (((1,), (1,)), ((), ())),
                        preferred_element_type=F32,
                    )
            lanes = slice(p1 * 2 * LANES, (p1 + 1) * 2 * LANES)
            total = jnp.concatenate([both[:, :LANES], both[:, LANES:] + odd], axis=1)
            hidden_ref[:, lanes] = total + bias_row

    fixed = lambda *shape: pl.BlockSpec(shape, lambda i: (0,) * len(shape))
    out_specs = [pl.BlockSpec((rows, 512), lambda i: (i, 0))]
    out_shape = [jax.ShapeDtypeStruct((count * rows, 512), F32)]
    if lead:
        out_specs += [fixed(FIELDS * own, slots * FIELDS), fixed(2 * LANES, 512)]
        out_shape += [
            jax.ShapeDtypeStruct((FIELDS * own, slots * FIELDS), BF16),
            jax.ShapeDtypeStruct((2 * LANES, 512), BF16),
        ]
    return pl.pallas_call(
        body,
        grid=(count,),
        in_specs=[
            pl.BlockSpec(memory_space=pltpu.SMEM),
            fixed(FIELDS, C_OUT),
            fixed(CELLS, own, C_IN),
            fixed(TAPS, C_OUT, C_IN),
            fixed(1, C_OUT),
        ],
        out_specs=out_specs,
        out_shape=out_shape,
        scratch_shapes=[pltpu.VMEM((2, 9, LANES, C_IN), BF16)],
        cost_estimate=pl.CostEstimate(
            flops=count * 2 * rows * C_IN * 3600, transcendentals=0, bytes_accessed=4 << 20
        ),
        compiler_params=pltpu.CompilerParams(vmem_limit_bytes=16 << 20),
        name="forward_part",
    )(destination, head, patches, weights, bias)


def split_sums(sums):
    high = sums.astype(BF16).astype(F32)
    return jnp.concatenate([high, sums - high], axis=0)


def backward(core, pick, arrived, head_table, cells, hidden):
    slots = cells.shape[1]
    span = 16 * slots
    rows = 4 * span
    groups = C_IN // 32

    def body(
        core_ref, pick_ref, arrived_ref, head_ref, x_ref, hidden_ref, keep_ref, send_ref, grad_ref, pack_ref
    ):
        lane = lax.broadcasted_iota(jnp.int32, (1, LANES), 1)
        chosen = jnp.dot(pick_ref[...], arrived_ref[...], preferred_element_type=F32).astype(BF16)
        turn = turn_terms()
        turned = [
            jnp.dot(chosen[:, m1 * LANES : (m1 + 1) * LANES], turn, preferred_element_type=F32)
            for m1 in range(4)
        ]
        pieces = []
        for j in range(16):
            piece = jnp.zeros((slots, LANES), F32)
            for f in range(FIELDS):
                part = turned[j // 4][f * slots : (f + 1) * slots]
                shift = (f - j % 4) * 32 % LANES
                part = pltpu.roll(part, shift, 1) if shift else part
                piece = jnp.where(lane // 32 == f, part, piece)
            pieces.append(piece.astype(BF16))
        fields = jnp.concatenate(pieces, axis=0)
        low_lanes = lane < C_OUT
        bias_sum = jnp.zeros((1, 512), F32)
        head_sum = jnp.zeros((LANES, 512), F32)
        for m3 in range(4):
            here = [slice((j * 4 + m3) * slots, (j * 4 + m3 + 1) * slots) for j in range(16)]
            mine = (lane // 2) % 4 == m3
            some = jnp.where(mine, fields, jnp.zeros_like(fields))
            upstream = jnp.dot(
                jnp.concatenate([some, some], axis=1), head_ref[...], preferred_element_type=F32
            )
            hidden = jnp.concatenate([hidden_ref[rows_of, :] for rows_of in here], axis=0)
            gate = jax.nn.sigmoid(hidden)
            active = hidden * gate
            grad = upstream * (gate * (1.0 + hidden * (1.0 - gate)))
            bias_sum = bias_sum + jnp.sum(grad, axis=0, keepdims=True)
            low = grad.astype(BF16)
            for j, rows_of in enumerate(here):
                grad_ref[rows_of, :] = low[j * slots : (j + 1) * slots]
            blk = [grad[:, b * LANES : (b + 1) * LANES] for b in range(4)]
            for k, (lo, hi) in enumerate(((0, 2), (1, 3), (2, 3))):
                packed = jnp.where(low_lanes, pltpu.roll(blk[lo], C_OUT, 1), blk[hi])
                packed = packed.astype(BF16)
                for j, rows_of in enumerate(here):
                    pack_ref[rows_of, k * LANES : (k + 1) * LANES] = packed[j * slots : (j + 1) * slots]
            high = active.astype(BF16)
            for term in (high, (active - high.astype(F32)).astype(BF16)):
                head_sum = head_sum + lax.dot_general(
                    some, term, (((0,), (0,)), ((), ())), preferred_element_type=F32
                )
        row = lax.broadcasted_iota(jnp.int32, (LANES, 512), 0)
        col = lax.broadcasted_iota(jnp.int32, (LANES, 512), 1)
        head_sum = jnp.where((row // 8 % 4) * 2 + row % 2 == col // C_OUT, head_sum, 0.0)
        heads = [
            jnp.sum(head_sum[f * 32 : (f + 1) * 32], axis=0, keepdims=True) for f in range(FIELDS)
        ]
        stacked = jnp.concatenate([bias_sum] + heads + [jnp.zeros((3, 512), F32)], axis=0)
        folded = sum(stacked[:, b * LANES : (b + 1) * LANES] for b in range(4))
        folded = folded + pltpu.roll(folded, C_OUT, 1)
        tail = split_sums(folded)
        mine_core = core_ref[0]

        def product(shift, at_ref, lanes):
            s1, s2, s3 = shift // 4, (shift // 2) % 2, shift % 2
            pieces = []
            for m in range(16):
                cell = (m // 4 + s1) * 25 + (m % 4 + s2) * 5 + s3
                pieces.append(x_ref[cell : cell + 4].reshape(4 * slots, C_IN))
            return lax.dot_general(
                jnp.concatenate(pieces, axis=0),
                at_ref[:, lanes],
                (((0,), (0,)), ((), ())),
                preferred_element_type=F32,
            )

        def put(block, value):
            split = value.reshape(groups, 2, 16, LANES)
            even, odd = split[:, 0], split[:, 1]
            if block == BLOCKS - 1:
                even, odd = (jnp.where(low_lanes[None], tail[None], half) for half in (even, odd))
            keep_ref[:, block * 16 : (block + 1) * 16, :] = jnp.where(mine_core == 0, even, odd)
            other = jnp.where(mine_core == 0, odd, even).astype(BF16)
            for g in range(groups):
                send_ref[(g * BLOCKS + block) * 16 : (g * BLOCKS + block + 1) * 16, :] = other[g]

        value = product(0, grad_ref, slice(0, 4 * LANES))
        for k, block in enumerate((4, 5, 7, 8)):
            put(block, value[:, k * LANES : (k + 1) * LANES])
        value = product(4, grad_ref, slice(2 * LANES, 4 * LANES))
        put(1, value[:, 0:LANES])
        put(2, value[:, LANES:])
        put(0, product(6, grad_ref, slice(3 * LANES, 4 * LANES)))
        value = product(2, grad_ref, slice(LANES, 4 * LANES))
        put(3, value[:, 0:LANES])
        put(6, value[:, 2 * LANES :])
        value = product(1, pack_ref, slice(0, 2 * LANES))
        put(9, value[:, 0:LANES])
        put(10, value[:, LANES:])
        put(11, product(3, pack_ref, slice(LANES, 2 * LANES)))
        put(12, product(5, pack_ref, slice(2 * LANES, 3 * LANES)))
        put(13, product(7, pack_ref, slice(LANES, 2 * LANES)))

    smem = pl.BlockSpec(memory_space=pltpu.SMEM)
    vmem = pl.BlockSpec(memory_space=pltpu.VMEM)
    return pl.pallas_call(
        body,
        in_specs=[smem] + [vmem] * 5,
        out_specs=[vmem, vmem],
        out_shape=[
            jax.ShapeDtypeStruct((groups, BLOCKS * 16, LANES), F32),
            jax.ShapeDtypeStruct((groups * BLOCKS * 16, LANES), BF16),
        ],
        scratch_shapes=[
            pltpu.VMEM((rows, 512), BF16),
            pltpu.VMEM((rows, 3 * LANES), BF16),
        ],
        compiler_params=pltpu.CompilerParams(vmem_limit_bytes=24 << 20),
        name="backward",
    )(core, pick, arrived, head_table, cells, hidden)


def pair_sum(keep, other):
    groups, block_rows, _ = keep.shape
    last = block_rows - 16

    def body(keep_ref, other_ref, out_ref):
        low_lanes = lax.broadcasted_iota(jnp.int32, (16, LANES), 1) < C_OUT
        for g in range(groups):
            partner = other_ref[g * block_rows : (g + 1) * block_rows, :].astype(F32)
            total = keep_ref[g] + partner
            out_ref[g, 0:last, :] = total[0:last].astype(BF16)
            tail = total[last:]
            tail = jnp.where(low_lanes, split_sums(tail[0:8] + tail[8:16]), tail)
            out_ref[g, last:, :] = tail.astype(BF16)

    return pl.pallas_call(
        body,
        out_shape=jax.ShapeDtypeStruct((groups, block_rows, LANES), BF16),
        compiler_params=pltpu.CompilerParams(vmem_limit_bytes=8 << 20),
        name="pair_sum",
    )(keep, other)


def final_sum(arrived, scale, per_block):
    sources = arrived.shape[0]

    def body(in_ref, conv_ref, bias_ref, head_ref):
        total = in_ref[0].astype(F32)
        for source in range(1, sources):
            total = total + in_ref[source].astype(F32)
        total = total * scale
        for block, taps in enumerate(HALF_TAPS):
            value = total[block * per_block : (block + 1) * per_block]
            for half, tap in enumerate(taps):
                if tap is not None:
                    conv_ref[tap] = value[:, half * C_OUT : (half + 1) * C_OUT]
        joined = value[0:8] + value[8:16]
        bias_ref[...] = joined[0:1, 0:C_OUT]
        head_ref[...] = joined[1 : 1 + FIELDS, 0:C_OUT]

    return pl.pallas_call(
        body,
        out_shape=[
            jax.ShapeDtypeStruct((TAPS, per_block, C_OUT), F32),
            jax.ShapeDtypeStruct((1, C_OUT), F32),
            jax.ShapeDtypeStruct((FIELDS, C_OUT), F32),
        ],
        compiler_params=pltpu.CompilerParams(vmem_limit_bytes=4 << 20),
        name="final_sum",
    )(arrived)


def on_device(patches, destination, cotangent, conv_weight, conv_bias, head_weight):
    owners = lax.axis_size("domain")
    my_index = lax.axis_index("domain")
    own_rows = patches.shape[0]
    train_rows = cotangent.shape[0]
    per_pair = (train_rows + owners - 1) // owners
    channels = C_IN // owners
    splits = 16 // channels
    if splits > 1:
        order = np.arange(C_IN).reshape(C_IN // 32, splits, 2, channels)
        order = order.transpose(0, 2, 1, 3).reshape(-1)
        patches = patches[:, :, order]
        conv_weight = conv_weight[order]

    listing = lax.all_to_all(
        spread(destination, owners),
        "domain",
        split_axis=0,
        concat_axis=0,
        tiled=True,
    )
    cells = patches.transpose(1, 0, 2)
    weights = conv_weight.transpose(1, 2, 0)
    slots = owners * per_pair
    bias = conv_bias.reshape(1, C_OUT)
    hidden, pick, head_table = forward_part(
        cells, 0, 4, weights, bias, destination, head_weight.T, slots, per_pair
    )
    me = my_index.astype(jnp.int32).reshape(1)
    rows = cotangent.reshape(train_rows * FIELDS, FINE)
    outgoing = row_copy(listing, me, rows, per_pair)
    arrived = lax.all_to_all(
        outgoing.reshape(owners, per_pair * FIELDS, FINE), "domain", split_axis=0, concat_axis=0, tiled=True
    ).reshape(owners * per_pair * FIELDS, FINE)

    core = (my_index % 2).astype(jnp.int32).reshape(1)
    keep, send = backward(core, pick, arrived, head_table, cells, hidden)
    other = lax.ppermute(send, "domain", [(i, i ^ 1) for i in range(owners)])
    payload = pair_sum(keep, other)

    scale = float((owners * own_rows * PS**3) ** (-0.5))
    mates = owners // 2
    groups = [[core_id + 2 * k for k in range(mates)] for core_id in range(2)]
    block_rows = BLOCKS * 16
    if splits > 1:
        tail = jnp.repeat(payload[:, block_rows - 16 :], splits, axis=0)
        blocks = payload.reshape(C_IN // 32, BLOCKS, splits, channels, LANES)
        blocks = blocks.transpose(0, 2, 1, 3, 4).reshape(mates, BLOCKS * channels, LANES)
        payload = jnp.concatenate([blocks, tail], axis=1)
    swapped = lax.all_to_all(
        payload, "domain", split_axis=0, concat_axis=0, tiled=True, axis_index_groups=groups
    )
    if splits > 1:
        tail = jnp.sum(swapped[:, BLOCKS * channels :].astype(F32), axis=0) * scale
        tail = tail[0:8, 0:C_OUT] + tail[8:, 0:C_OUT]
        total = jnp.sum(swapped[:, : BLOCKS * channels].astype(F32), axis=0) * scale
        total = total.reshape(BLOCKS, channels, 2, C_OUT)
        where = {tap: (b, h) for b, pair in enumerate(HALF_TAPS) for h, tap in enumerate(pair)}
        conv = jnp.stack([total[where[t][0], :, where[t][1]] for t in range(TAPS)], axis=1)
        return conv, tail[0], tail[1 : 1 + FIELDS].T
    conv, bias_out, head_out = final_sum(swapped, scale, channels)
    return conv.transpose(1, 0, 2), bias_out.reshape(C_OUT), head_out.T


def solution(mesh):
    placed = (
        P(("groups", "domain"), None, None),
        P(("groups", "domain")),
        P(("groups", "domain"), None, None),
        P(),
        P(),
        P(),
    )
    return jax.shard_map(
        on_device,
        mesh=mesh,
        in_specs=placed,
        out_specs=(P(("groups", "domain"), None, None), P("groups"), P("groups", None)),
        check_vma=False,
    )
```

```python
import jax
import jax.numpy as jnp
import numpy as np
from jax import lax
from jax.experimental import pallas as pl
from jax.experimental.pallas import tpu as pltpu
from jax.sharding import PartitionSpec as P

C_IN = 256
C_OUT = 64
FIELDS = 4
TAPS = 27
PS = 4
PAD = 5
CELLS = PAD**3
FINE = 512
LANES = 128
BLOCKS = 14
SEND_ORDER = (4, 6, 5, 7, 1, 3, 2)
F32 = jnp.float32
BF16 = jnp.bfloat16
HALF_TAPS = [(b * 3 + 1, b * 3 + 2) for b in range(9)]
HALF_TAPS += [(4 * 3, 7 * 3), (5 * 3, 8 * 3), (3 * 3, 6 * 3), (1 * 3, 2 * 3), (None, 0)]


def row_copy(listing, me, rows, per_pair):
    owners, _, own = listing.shape
    lines = owners * per_pair * FIELDS

    def body(me_ref, listing_ref, rows_ref, out_ref):
        hits = (listing_ref[...].reshape(owners, own) == me_ref[0]).astype(F32)
        counts = jnp.broadcast_to(jnp.sum(hits, axis=1, keepdims=True), (owners, LANES)).astype(BF16)
        line = lax.broadcasted_iota(jnp.int32, (lines, owners), 0)
        owner = lax.broadcasted_iota(jnp.int32, (lines, owners), 1)
        before = (owner < line // (per_pair * FIELDS)).astype(F32).astype(BF16)
        starts = jnp.dot(before, counts, preferred_element_type=F32)
        line = lax.broadcasted_iota(jnp.int32, (lines, LANES), 0)
        lane = lax.broadcasted_iota(jnp.int32, (lines, LANES), 1)
        wanted = starts.astype(jnp.int32) * FIELDS + line % (per_pair * FIELDS)
        pick = (wanted == lane).astype(F32).astype(BF16)
        out_ref[...] = jnp.dot(pick, rows_ref[...], preferred_element_type=F32).astype(BF16)

    vmem = pl.BlockSpec(memory_space=pltpu.VMEM)
    return pl.pallas_call(
        body,
        in_specs=[pl.BlockSpec(memory_space=pltpu.SMEM), vmem, vmem],
        out_specs=vmem,
        out_shape=jax.ShapeDtypeStruct((lines, FINE), BF16),
        compiler_params=pltpu.CompilerParams(vmem_limit_bytes=4 << 20),
        cost_estimate=pl.CostEstimate(flops=8 << 30, transcendentals=0, bytes_accessed=1 << 20),
        name="row_copy",
    )(me, listing, rows)


def spread(destination, owners):
    own = destination.shape[0]

    def body(in_ref, out_ref):
        out_ref[...] = jnp.broadcast_to(in_ref[...].reshape(1, 1, own), (owners, 1, own))

    return pl.pallas_call(
        body, out_shape=jax.ShapeDtypeStruct((owners, 1, own), jnp.int32), name="spread"
    )(destination.reshape(1, own))


def turn_terms():
    fine = lax.broadcasted_iota(jnp.int32, (LANES, LANES), 0)
    lane = lax.broadcasted_iota(jnp.int32, (LANES, LANES), 1)
    to = ((fine >> 4) & 3) * 32 + (fine >> 6) * 16 + (fine & 15)
    return (to == lane).astype(F32).astype(BF16)


def head_terms(head):
    rows = jnp.concatenate([jnp.broadcast_to(head[f : f + 1], (32, C_OUT)) for f in range(FIELDS)], axis=0)
    pair = jnp.concatenate([rows, rows], axis=1)
    table = jnp.concatenate([pair] * 4, axis=1)
    row = lax.broadcasted_iota(jnp.int32, table.shape, 0)
    col = lax.broadcasted_iota(jnp.int32, table.shape, 1)
    table = jnp.where((row // 8 % 4) * 2 + row % 2 == col // C_OUT, table, 0.0)
    high = table.astype(BF16)
    return jnp.concatenate([high, (table - high.astype(F32)).astype(BF16)], axis=0)


def forward_part(patches, first, count, weights, bias, destination, head, slots, per_pair):
    own = patches.shape[1]
    rows = 16 * own
    lead = first == 0

    def body(*refs):
        dest_ref, head_ref, x_ref, w_ref, bias_ref = refs[:5]
        hidden_ref = refs[5]
        w2_ref = refs[-1]
        step = pl.program_id(0)

        @pl.when(step == 0)
        def _():
            w2_ref[1, :, 0:C_OUT, :] = jnp.zeros((9, C_OUT, C_IN), BF16)
            for b in range(9):
                w2_ref[0, b] = w_ref[3 * b + 1 : 3 * b + 3].reshape(2 * C_OUT, C_IN)
                w2_ref[1, b, C_OUT:, :] = w_ref[3 * b]
            if lead:
                pick_ref, table_ref = refs[6:8]
                line = lax.broadcasted_iota(jnp.int32, (FIELDS * own, slots * FIELDS), 0)
                lane = lax.broadcasted_iota(jnp.int32, (FIELDS * own, slots * FIELDS), 1)
                wanted = jnp.zeros_like(line)
                for n in range(own):
                    rank = jnp.int32(0)
                    for k in range(n):
                        rank = rank + (dest_ref[k] == dest_ref[n]).astype(jnp.int32)
                    wanted = jnp.where(line % own == n, dest_ref[n] * per_pair + rank, wanted)
                wanted = wanted * FIELDS + line // own
                pick_ref[...] = (wanted == lane).astype(F32).astype(BF16)
                table_ref[...] = head_terms(head_ref[...])

        m1 = step + first
        picked = []
        for shift in range(8):
            s1, s2, s3 = shift // 4, (shift // 2) % 2, shift % 2
            pieces = [
                x_ref[pl.ds((m1 + s1) * 25 + (m2 + s2) * 5 + s3, 4)].reshape(4 * own, C_IN)
                for m2 in range(4)
            ]
            picked.append(jnp.concatenate(pieces, axis=0))
        bias_row = jnp.concatenate([bias_ref[...]] * 4, axis=1)
        for p1 in range(2):
            both = jnp.zeros((rows, 2 * LANES), F32)
            odd = jnp.zeros((rows, LANES), F32)
            for s1 in range(p1 + 1):
                k1 = 1 if p1 == 0 else (2 if s1 == 0 else 0)
                for s3 in range(2):
                    both = both + lax.dot_general(
                        picked[s1 * 4 + s3],
                        w2_ref[s3, k1 * 3 + 1 : k1 * 3 + 3].reshape(2 * LANES, C_IN),
                        (((1,), (1,)), ((), ())),
                        preferred_element_type=F32,
                    )
                    odd = odd + lax.dot_general(
                        picked[s1 * 4 + 2 + s3],
                        w2_ref[s3, k1 * 3],
                        (((1,), (1,)), ((), ())),
                        preferred_element_type=F32,
                    )
            lanes = slice(p1 * 2 * LANES, (p1 + 1) * 2 * LANES)
            total = jnp.concatenate([both[:, :LANES], both[:, LANES:] + odd], axis=1)
            hidden_ref[:, lanes] = total + bias_row

    fixed = lambda *shape: pl.BlockSpec(shape, lambda i: (0,) * len(shape))
    out_specs = [pl.BlockSpec((rows, 512), lambda i: (i, 0))]
    out_shape = [jax.ShapeDtypeStruct((count * rows, 512), F32)]
    if lead:
        out_specs += [fixed(FIELDS * own, slots * FIELDS), fixed(2 * LANES, 512)]
        out_shape += [
            jax.ShapeDtypeStruct((FIELDS * own, slots * FIELDS), BF16),
            jax.ShapeDtypeStruct((2 * LANES, 512), BF16),
        ]
    return pl.pallas_call(
        body,
        grid=(count,),
        in_specs=[
            pl.BlockSpec(memory_space=pltpu.SMEM),
            fixed(FIELDS, C_OUT),
            fixed(CELLS, own, C_IN),
            fixed(TAPS, C_OUT, C_IN),
            fixed(1, C_OUT),
        ],
        out_specs=out_specs,
        out_shape=out_shape,
        scratch_shapes=[pltpu.VMEM((2, 9, LANES, C_IN), BF16)],
        cost_estimate=pl.CostEstimate(
            flops=count * 2 * rows * C_IN * 3600, transcendentals=0, bytes_accessed=4 << 20
        ),
        compiler_params=pltpu.CompilerParams(vmem_limit_bytes=16 << 20),
        name="forward_part",
    )(destination, head, patches, weights, bias)


def split_sums(sums):
    high = sums.astype(BF16).astype(F32)
    return jnp.concatenate([high, sums - high], axis=0)


def backward(me, pick, arrived, head_table, cells, hidden, direct):
    slots = cells.shape[1]
    span = 16 * slots
    rows = 4 * span
    groups = C_IN // 32

    def body(
        me_ref, pick_ref, arrived_ref, head_ref, x_ref, hidden_ref, keep_ref, send_ref, grad_ref, pack_ref
    ):
        lane = lax.broadcasted_iota(jnp.int32, (1, LANES), 1)
        chosen = jnp.dot(pick_ref[...], arrived_ref[...], preferred_element_type=F32).astype(BF16)
        turn = turn_terms()
        turned = [
            jnp.dot(chosen[:, m1 * LANES : (m1 + 1) * LANES], turn, preferred_element_type=F32)
            for m1 in range(4)
        ]
        pieces = []
        for j in range(16):
            piece = jnp.zeros((slots, LANES), F32)
            for f in range(FIELDS):
                part = turned[j // 4][f * slots : (f + 1) * slots]
                shift = (f - j % 4) * 32 % LANES
                part = pltpu.roll(part, shift, 1) if shift else part
                piece = jnp.where(lane // 32 == f, part, piece)
            pieces.append(piece.astype(BF16))
        fields = jnp.concatenate(pieces, axis=0)
        low_lanes = lane < C_OUT
        bias_sum = jnp.zeros((1, 512), F32)
        head_sum = jnp.zeros((LANES, 512), F32)
        for m3 in range(4):
            here = [slice((j * 4 + m3) * slots, (j * 4 + m3 + 1) * slots) for j in range(16)]
            mine = (lane // 2) % 4 == m3
            some = jnp.where(mine, fields, jnp.zeros_like(fields))
            upstream = jnp.dot(
                jnp.concatenate([some, some], axis=1), head_ref[...], preferred_element_type=F32
            )
            hidden = jnp.concatenate([hidden_ref[rows_of, :] for rows_of in here], axis=0)
            gate = jax.nn.sigmoid(hidden)
            active = hidden * gate
            grad = upstream * (gate * (1.0 + hidden * (1.0 - gate)))
            bias_sum = bias_sum + jnp.sum(grad, axis=0, keepdims=True)
            low = grad.astype(BF16)
            for j, rows_of in enumerate(here):
                grad_ref[rows_of, :] = low[j * slots : (j + 1) * slots]
            blk = [grad[:, b * LANES : (b + 1) * LANES] for b in range(4)]
            for k, (lo, hi) in enumerate(((0, 2), (1, 3), (2, 3))):
                packed = jnp.where(low_lanes, pltpu.roll(blk[lo], C_OUT, 1), blk[hi])
                packed = packed.astype(BF16)
                for j, rows_of in enumerate(here):
                    pack_ref[rows_of, k * LANES : (k + 1) * LANES] = packed[j * slots : (j + 1) * slots]
            high = active.astype(BF16)
            for term in (high, (active - high.astype(F32)).astype(BF16)):
                head_sum = head_sum + lax.dot_general(
                    some, term, (((0,), (0,)), ((), ())), preferred_element_type=F32
                )
        row = lax.broadcasted_iota(jnp.int32, (LANES, 512), 0)
        col = lax.broadcasted_iota(jnp.int32, (LANES, 512), 1)
        head_sum = jnp.where((row // 8 % 4) * 2 + row % 2 == col // C_OUT, head_sum, 0.0)
        heads = [
            jnp.sum(head_sum[f * 32 : (f + 1) * 32], axis=0, keepdims=True) for f in range(FIELDS)
        ]
        stacked = jnp.concatenate([bias_sum] + heads + [jnp.zeros((3, 512), F32)], axis=0)
        folded = sum(stacked[:, b * LANES : (b + 1) * LANES] for b in range(4))
        folded = folded + pltpu.roll(folded, C_OUT, 1)
        tail = split_sums(folded)
        first_core = (me_ref[0] & 1) == 0
        home = me_ref[0] >> 1 if direct else 0

        def product(shift, value):
            s1, s2, s3 = shift // 4, (shift // 2) % 2, shift % 2
            pieces = []
            for m in range(16):
                cell = (m // 4 + s1) * 25 + (m % 4 + s2) * 5 + s3
                pieces.append(x_ref[cell : cell + 4].reshape(4 * slots, C_IN))
            return lax.dot_general(
                jnp.concatenate(pieces, axis=0),
                value,
                (((0,), (0,)), ((), ())),
                preferred_element_type=F32,
            )

        def put(block, value):
            split = value.reshape(groups, 2, 16, LANES)
            even, odd = split[:, 0], split[:, 1]
            if block == BLOCKS - 1:
                even, odd = (jnp.where(low_lanes[None], tail[None], half) for half in (even, odd))
            mine = jnp.where(first_core, even, odd)
            other = jnp.where(first_core, odd, even).astype(BF16)
            at = slice(block * 16, (block + 1) * 16)
            for g in range(groups):
                keep_ref[g ^ home, at, :] = mine[g]
                send_ref[g ^ home, at, :] = other[g]

        def put_pair(blocks, value):
            put(blocks[0], value[:, 0:LANES])
            put(blocks[1], value[:, LANES : 2 * LANES])

        grads = [grad_ref[:, b * LANES : (b + 1) * LANES] for b in range(4)]
        packs = [pack_ref[:, b * LANES : (b + 1) * LANES] for b in range(3)]
        join = lambda *parts: jnp.concatenate(parts, axis=1)
        value = product(0, join(*grads))
        put_pair((4, 5), value[:, : 2 * LANES])
        put_pair((7, 8), value[:, 2 * LANES :])
        put_pair((1, 2), product(4, join(grads[2], grads[3])))
        put_pair((3, 6), product(2, join(grads[1], grads[3])))
        put(0, product(6, grads[3]))
        put_pair((9, 10), product(1, join(packs[0], packs[1])))
        put(11, product(3, packs[1]))
        put(12, product(5, packs[2]))
        put(13, product(7, packs[1]))

    vmem = pl.BlockSpec(memory_space=pltpu.VMEM)
    return pl.pallas_call(
        body,
        in_specs=[pl.BlockSpec(memory_space=pltpu.SMEM)] + [vmem] * 5,
        out_specs=[vmem, vmem],
        out_shape=[
            jax.ShapeDtypeStruct((groups, BLOCKS * 16, LANES), F32),
            jax.ShapeDtypeStruct((groups, BLOCKS * 16, LANES), BF16),
        ],
        scratch_shapes=[
            pltpu.VMEM((rows, 512), BF16),
            pltpu.VMEM((rows, 3 * LANES), BF16),
        ],
        compiler_params=pltpu.CompilerParams(vmem_limit_bytes=24 << 20),
        name="backward",
    )(me, pick, arrived, head_table, cells, hidden)


def pair_sum(keep, other, direct):
    groups, block_rows, _ = keep.shape
    last = block_rows - 16

    def body(keep_ref, other_ref, *out_refs):
        low_lanes = lax.broadcasted_iota(jnp.int32, (16, LANES), 1) < C_OUT
        for g in range(groups):
            out_ref = out_refs[g] if direct else out_refs[0].at[g]
            total = keep_ref[g] + other_ref[g].astype(F32)
            tail = total[last:]
            tail = jnp.where(low_lanes, split_sums(tail[0:8] + tail[8:16]), tail)
            out_ref[0:last, :] = total[0:last].astype(out_ref.dtype)
            out_ref[last:, :] = tail.astype(out_ref.dtype)

    if direct:
        out_shape = [
            jax.ShapeDtypeStruct((block_rows, LANES), BF16 if g else F32) for g in range(groups)
        ]
    else:
        out_shape = [jax.ShapeDtypeStruct((groups, block_rows, LANES), BF16)]
    return pl.pallas_call(
        body,
        out_shape=out_shape,
        compiler_params=pltpu.CompilerParams(vmem_limit_bytes=8 << 20),
        name="pair_sum",
    )(keep, other)


def final_sum(arrived, scale, per_block):
    def body(*refs):
        conv_ref, bias_ref, head_ref = refs[len(arrived) :]
        total = refs[0][...]
        for ref in refs[1 : len(arrived)]:
            total = total + ref[...].astype(F32)
        total = total * scale
        for block, taps in enumerate(HALF_TAPS):
            value = total[block * per_block : (block + 1) * per_block]
            for half, tap in enumerate(taps):
                if tap is not None:
                    conv_ref[tap] = value[:, half * C_OUT : (half + 1) * C_OUT]
        joined = value[0:8] + value[8:16]
        bias_ref[...] = joined[0:1, 0:C_OUT]
        head_ref[...] = joined[1 : 1 + FIELDS, 0:C_OUT]

    return pl.pallas_call(
        body,
        out_shape=[
            jax.ShapeDtypeStruct((TAPS, per_block, C_OUT), F32),
            jax.ShapeDtypeStruct((1, C_OUT), F32),
            jax.ShapeDtypeStruct((FIELDS, C_OUT), F32),
        ],
        compiler_params=pltpu.CompilerParams(vmem_limit_bytes=4 << 20),
        name="final_sum",
    )(*arrived)


def on_device(patches, destination, cotangent, conv_weight, conv_bias, head_weight):
    owners = lax.axis_size("domain")
    my_index = lax.axis_index("domain")
    own_rows = patches.shape[0]
    train_rows = cotangent.shape[0]
    per_pair = (train_rows + owners - 1) // owners
    channels = C_IN // owners
    splits = 16 // channels
    if splits > 1:
        order = np.arange(C_IN).reshape(C_IN // 32, splits, 2, channels)
        order = order.transpose(0, 2, 1, 3).reshape(-1)
        patches = patches[:, :, order]
        conv_weight = conv_weight[order]

    listing = lax.all_to_all(
        spread(destination, owners),
        "domain",
        split_axis=0,
        concat_axis=0,
        tiled=True,
    )
    cells = patches.transpose(1, 0, 2)
    weights = conv_weight.transpose(1, 2, 0)
    slots = owners * per_pair
    bias = conv_bias.reshape(1, C_OUT)
    hidden, pick, head_table = forward_part(
        cells, 0, 4, weights, bias, destination, head_weight.T, slots, per_pair
    )
    me = my_index.astype(jnp.int32).reshape(1)
    rows = cotangent.reshape(train_rows * FIELDS, FINE)
    outgoing = row_copy(listing, me, rows, per_pair)
    arrived = lax.all_to_all(
        outgoing.reshape(owners, per_pair * FIELDS, FINE), "domain", split_axis=0, concat_axis=0, tiled=True
    ).reshape(owners * per_pair * FIELDS, FINE)

    mates = owners // 2
    direct = mates == C_IN // 32
    keep, send = backward(me, pick, arrived, head_table, cells, hidden, direct)
    other = lax.ppermute(send, "domain", [(i, i ^ 1) for i in range(owners)])
    payload = pair_sum(keep, other, direct)

    scale = float((owners * own_rows * PS**3) ** (-0.5))
    if direct:
        arrived = [payload[0]]
        for k in SEND_ORDER:
            arrived.append(lax.ppermute(payload[k], "domain", [(i, i ^ (2 * k)) for i in range(owners)]))
        conv, bias_out, head_out = final_sum(arrived, scale, channels)
        return conv.transpose(1, 0, 2), bias_out.reshape(C_OUT), head_out.T
    groups = [[core_id + 2 * k for k in range(mates)] for core_id in range(2)]
    tail = jnp.repeat(payload[0][:, (BLOCKS - 1) * 16 :], splits, axis=0)
    blocks = payload[0].reshape(C_IN // 32, BLOCKS, splits, channels, LANES)
    blocks = blocks.transpose(0, 2, 1, 3, 4).reshape(mates, BLOCKS * channels, LANES)
    swapped = lax.all_to_all(
        jnp.concatenate([blocks, tail], axis=1),
        "domain",
        split_axis=0,
        concat_axis=0,
        tiled=True,
        axis_index_groups=groups,
    )
    total = jnp.sum(swapped.astype(F32), axis=0) * scale
    tail = total[BLOCKS * channels :, 0:C_OUT]
    tail = tail[0:8] + tail[8:]
    total = total[: BLOCKS * channels].reshape(BLOCKS, channels, 2, C_OUT)
    where = {tap: (b, h) for b, pair in enumerate(HALF_TAPS) for h, tap in enumerate(pair)}
    conv = jnp.stack([total[where[t][0], :, where[t][1]] for t in range(TAPS)], axis=1)
    return conv, tail[0], tail[1 : 1 + FIELDS].T


def solution(mesh):
    placed = (
        P(("groups", "domain"), None, None),
        P(("groups", "domain")),
        P(("groups", "domain"), None, None),
        P(),
        P(),
        P(),
    )
    return jax.shard_map(
        on_device,
        mesh=mesh,
        in_specs=placed,
        out_specs=(P(("groups", "domain"), None, None), P("groups"), P("groups", None)),
        check_vma=False,
    )
```

```python
import jax
import jax.numpy as jnp
import numpy as np
from jax import lax
from jax.experimental import pallas as pl
from jax.experimental.pallas import tpu as pltpu
from jax.sharding import PartitionSpec as P

C_IN = 256
C_OUT = 64
FIELDS = 4
TAPS = 27
PS = 4
PAD = 5
CELLS = PAD**3
FINE = 512
LANES = 128
BLOCKS = 14
SEND_ORDER = (4, 7, 5, 6, 2, 3, 1)
F32 = jnp.float32
BF16 = jnp.bfloat16
HALF_TAPS = [(b * 3 + 1, b * 3 + 2) for b in range(9)]
HALF_TAPS += [(4 * 3, 7 * 3), (5 * 3, 8 * 3), (3 * 3, 6 * 3), (1 * 3, 2 * 3), (None, 0)]


def row_copy(listing, me, rows, per_pair):
    owners, _, own = listing.shape
    lines = owners * per_pair * FIELDS

    def body(me_ref, listing_ref, rows_ref, out_ref):
        hits = (listing_ref[...].reshape(owners, own) == me_ref[0]).astype(F32)
        counts = jnp.broadcast_to(jnp.sum(hits, axis=1, keepdims=True), (owners, LANES)).astype(BF16)
        line = lax.broadcasted_iota(jnp.int32, (lines, owners), 0)
        owner = lax.broadcasted_iota(jnp.int32, (lines, owners), 1)
        before = (owner < line // (per_pair * FIELDS)).astype(F32).astype(BF16)
        starts = jnp.dot(before, counts, preferred_element_type=F32)
        line = lax.broadcasted_iota(jnp.int32, (lines, LANES), 0)
        lane = lax.broadcasted_iota(jnp.int32, (lines, LANES), 1)
        wanted = starts.astype(jnp.int32) * FIELDS + line % (per_pair * FIELDS)
        pick = (wanted == lane).astype(F32).astype(BF16)
        out_ref[...] = jnp.dot(pick, rows_ref[...], preferred_element_type=F32).astype(BF16)

    vmem = pl.BlockSpec(memory_space=pltpu.VMEM)
    return pl.pallas_call(
        body,
        in_specs=[pl.BlockSpec(memory_space=pltpu.SMEM), vmem, vmem],
        out_specs=vmem,
        out_shape=jax.ShapeDtypeStruct((lines, FINE), BF16),
        compiler_params=pltpu.CompilerParams(vmem_limit_bytes=4 << 20),
        cost_estimate=pl.CostEstimate(flops=8 << 30, transcendentals=0, bytes_accessed=1 << 20),
        name="row_copy",
    )(me, listing, rows)


def spread(destination, owners):
    own = destination.shape[0]

    def body(in_ref, out_ref):
        out_ref[...] = jnp.broadcast_to(in_ref[...].reshape(1, 1, own), (owners, 1, own))

    return pl.pallas_call(
        body, out_shape=jax.ShapeDtypeStruct((owners, 1, own), jnp.int32), name="spread"
    )(destination.reshape(1, own))


def turn_terms():
    fine = lax.broadcasted_iota(jnp.int32, (LANES, LANES), 0)
    lane = lax.broadcasted_iota(jnp.int32, (LANES, LANES), 1)
    to = ((fine >> 4) & 3) * 32 + (fine >> 6) * 16 + (fine & 15)
    return (to == lane).astype(F32).astype(BF16)


def head_terms(head):
    rows = jnp.concatenate([jnp.broadcast_to(head[f : f + 1], (32, C_OUT)) for f in range(FIELDS)], axis=0)
    pair = jnp.concatenate([rows, rows], axis=1)
    table = jnp.concatenate([pair] * 4, axis=1)
    row = lax.broadcasted_iota(jnp.int32, table.shape, 0)
    col = lax.broadcasted_iota(jnp.int32, table.shape, 1)
    table = jnp.where((row // 8 % 4) * 2 + row % 2 == col // C_OUT, table, 0.0)
    high = table.astype(BF16)
    return jnp.concatenate([high, (table - high.astype(F32)).astype(BF16)], axis=0)


def forward_part(patches, first, count, weights, bias, destination, head, slots, per_pair):
    own = patches.shape[1]
    rows = 16 * own
    lead = first == 0

    def body(*refs):
        dest_ref, head_ref, x_ref, w_ref, bias_ref = refs[:5]
        hidden_ref = refs[5]
        w2_ref = refs[-1]
        step = pl.program_id(0)

        @pl.when(step == 0)
        def _():
            w2_ref[1, :, 0:C_OUT, :] = jnp.zeros((9, C_OUT, C_IN), BF16)
            for b in range(9):
                w2_ref[0, b] = w_ref[3 * b + 1 : 3 * b + 3].reshape(2 * C_OUT, C_IN)
                w2_ref[1, b, C_OUT:, :] = w_ref[3 * b]
            if lead:
                pick_ref, table_ref = refs[6:8]
                line = lax.broadcasted_iota(jnp.int32, (FIELDS * own, slots * FIELDS), 0)
                lane = lax.broadcasted_iota(jnp.int32, (FIELDS * own, slots * FIELDS), 1)
                wanted = jnp.zeros_like(line)
                for n in range(own):
                    rank = jnp.int32(0)
                    for k in range(n):
                        rank = rank + (dest_ref[k] == dest_ref[n]).astype(jnp.int32)
                    wanted = jnp.where(line % own == n, dest_ref[n] * per_pair + rank, wanted)
                wanted = wanted * FIELDS + line // own
                pick_ref[...] = (wanted == lane).astype(F32).astype(BF16)
                table_ref[...] = head_terms(head_ref[...])

        m1 = step + first
        picked = []
        for shift in range(8):
            s1, s2, s3 = shift // 4, (shift // 2) % 2, shift % 2
            pieces = [
                x_ref[pl.ds((m1 + s1) * 25 + (m2 + s2) * 5 + s3, 4)].reshape(4 * own, C_IN)
                for m2 in range(4)
            ]
            picked.append(jnp.concatenate(pieces, axis=0))
        bias_row = jnp.concatenate([bias_ref[...]] * 4, axis=1)
        for p1 in range(2):
            both = jnp.zeros((rows, 2 * LANES), F32)
            odd = jnp.zeros((rows, LANES), F32)
            for s1 in range(p1 + 1):
                k1 = 1 if p1 == 0 else (2 if s1 == 0 else 0)
                for s3 in range(2):
                    both = both + lax.dot_general(
                        picked[s1 * 4 + s3],
                        w2_ref[s3, k1 * 3 + 1 : k1 * 3 + 3].reshape(2 * LANES, C_IN),
                        (((1,), (1,)), ((), ())),
                        preferred_element_type=F32,
                    )
                    odd = odd + lax.dot_general(
                        picked[s1 * 4 + 2 + s3],
                        w2_ref[s3, k1 * 3],
                        (((1,), (1,)), ((), ())),
                        preferred_element_type=F32,
                    )
            lanes = slice(p1 * 2 * LANES, (p1 + 1) * 2 * LANES)
            total = jnp.concatenate([both[:, :LANES], both[:, LANES:] + odd], axis=1)
            hidden_ref[:, lanes] = total + bias_row

    fixed = lambda *shape: pl.BlockSpec(shape, lambda i: (0,) * len(shape))
    out_specs = [pl.BlockSpec((rows, 512), lambda i: (i, 0))]
    out_shape = [jax.ShapeDtypeStruct((count * rows, 512), F32)]
    if lead:
        out_specs += [fixed(FIELDS * own, slots * FIELDS), fixed(2 * LANES, 512)]
        out_shape += [
            jax.ShapeDtypeStruct((FIELDS * own, slots * FIELDS), BF16),
            jax.ShapeDtypeStruct((2 * LANES, 512), BF16),
        ]
    return pl.pallas_call(
        body,
        grid=(count,),
        in_specs=[
            pl.BlockSpec(memory_space=pltpu.SMEM),
            fixed(FIELDS, C_OUT),
            fixed(CELLS, own, C_IN),
            fixed(TAPS, C_OUT, C_IN),
            fixed(1, C_OUT),
        ],
        out_specs=out_specs,
        out_shape=out_shape,
        scratch_shapes=[pltpu.VMEM((2, 9, LANES, C_IN), BF16)],
        cost_estimate=pl.CostEstimate(
            flops=count * 2 * rows * C_IN * 3600, transcendentals=0, bytes_accessed=4 << 20
        ),
        compiler_params=pltpu.CompilerParams(vmem_limit_bytes=16 << 20),
        name="forward_part",
    )(destination, head, patches, weights, bias)


def split_sums(sums):
    high = sums.astype(BF16).astype(F32)
    return jnp.concatenate([high, sums - high], axis=0)


def backward(me, pick, arrived, head_table, cells, hidden, direct):
    slots = cells.shape[1]
    span = 16 * slots
    rows = 4 * span
    groups = C_IN // 32

    def body(
        me_ref, pick_ref, arrived_ref, head_ref, x_ref, hidden_ref, keep_ref, send_ref, grad_ref, pack_ref
    ):
        lane = lax.broadcasted_iota(jnp.int32, (1, LANES), 1)
        chosen = jnp.dot(pick_ref[...], arrived_ref[...], preferred_element_type=F32).astype(BF16)
        turn = turn_terms()
        turned = [
            jnp.dot(chosen[:, m1 * LANES : (m1 + 1) * LANES], turn, preferred_element_type=F32)
            for m1 in range(4)
        ]
        pieces = []
        for j in range(16):
            piece = jnp.zeros((slots, LANES), F32)
            for f in range(FIELDS):
                part = turned[j // 4][f * slots : (f + 1) * slots]
                shift = (f - j % 4) * 32 % LANES
                part = pltpu.roll(part, shift, 1) if shift else part
                piece = jnp.where(lane // 32 == f, part, piece)
            pieces.append(piece.astype(BF16))
        fields = jnp.concatenate(pieces, axis=0)
        low_lanes = lane < C_OUT
        bias_sum = jnp.zeros((1, 512), F32)
        head_sum = jnp.zeros((LANES, 512), F32)
        for m3 in range(4):
            here = [slice((j * 4 + m3) * slots, (j * 4 + m3 + 1) * slots) for j in range(16)]
            mine = (lane // 2) % 4 == m3
            some = jnp.where(mine, fields, jnp.zeros_like(fields))
            upstream = jnp.dot(
                jnp.concatenate([some, some], axis=1), head_ref[...], preferred_element_type=F32
            )
            hidden = jnp.concatenate([hidden_ref[rows_of, :] for rows_of in here], axis=0)
            gate = jax.nn.sigmoid(hidden)
            active = hidden * gate
            grad = upstream * (gate * (1.0 + hidden * (1.0 - gate)))
            bias_sum = bias_sum + jnp.sum(grad, axis=0, keepdims=True)
            low = grad.astype(BF16)
            for j, rows_of in enumerate(here):
                grad_ref[rows_of, :] = low[j * slots : (j + 1) * slots]
            blk = [grad[:, b * LANES : (b + 1) * LANES] for b in range(4)]
            for k, (lo, hi) in enumerate(((0, 2), (1, 3), (2, 3))):
                packed = jnp.where(low_lanes, pltpu.roll(blk[lo], C_OUT, 1), blk[hi])
                packed = packed.astype(BF16)
                for j, rows_of in enumerate(here):
                    pack_ref[rows_of, k * LANES : (k + 1) * LANES] = packed[j * slots : (j + 1) * slots]
            high = active.astype(BF16)
            for term in (high, (active - high.astype(F32)).astype(BF16)):
                head_sum = head_sum + lax.dot_general(
                    some, term, (((0,), (0,)), ((), ())), preferred_element_type=F32
                )
        row = lax.broadcasted_iota(jnp.int32, (LANES, 512), 0)
        col = lax.broadcasted_iota(jnp.int32, (LANES, 512), 1)
        head_sum = jnp.where((row // 8 % 4) * 2 + row % 2 == col // C_OUT, head_sum, 0.0)
        heads = [
            jnp.sum(head_sum[f * 32 : (f + 1) * 32], axis=0, keepdims=True) for f in range(FIELDS)
        ]
        stacked = jnp.concatenate([bias_sum] + heads + [jnp.zeros((3, 512), F32)], axis=0)
        folded = sum(stacked[:, b * LANES : (b + 1) * LANES] for b in range(4))
        folded = folded + pltpu.roll(folded, C_OUT, 1)
        tail = split_sums(folded)
        first_core = (me_ref[0] & 1) == 0
        home = me_ref[0] >> 1 if direct else 0

        def product(shift, value):
            s1, s2, s3 = shift // 4, (shift // 2) % 2, shift % 2
            pieces = []
            for m in range(16):
                cell = (m // 4 + s1) * 25 + (m % 4 + s2) * 5 + s3
                pieces.append(x_ref[cell : cell + 4].reshape(4 * slots, C_IN))
            return lax.dot_general(
                jnp.concatenate(pieces, axis=0),
                value,
                (((0,), (0,)), ((), ())),
                preferred_element_type=F32,
            )

        def put(block, value):
            split = value.reshape(groups, 2, 16, LANES)
            even, odd = split[:, 0], split[:, 1]
            if block == BLOCKS - 1:
                even, odd = (jnp.where(low_lanes[None], tail[None], half) for half in (even, odd))
            mine = jnp.where(first_core, even, odd)
            other = jnp.where(first_core, odd, even).astype(BF16)
            at = slice(block * 16, (block + 1) * 16)
            for g in range(groups):
                keep_ref[g ^ home, at, :] = mine[g]
                send_ref[g ^ home, at, :] = other[g]

        def put_pair(blocks, value):
            put(blocks[0], value[:, 0:LANES])
            put(blocks[1], value[:, LANES : 2 * LANES])

        grads = [grad_ref[:, b * LANES : (b + 1) * LANES] for b in range(4)]
        packs = [pack_ref[:, b * LANES : (b + 1) * LANES] for b in range(3)]
        join = lambda *parts: jnp.concatenate(parts, axis=1)
        value = product(0, join(*grads))
        put_pair((4, 5), value[:, : 2 * LANES])
        put_pair((7, 8), value[:, 2 * LANES :])
        put_pair((1, 2), product(4, join(grads[2], grads[3])))
        put_pair((3, 6), product(2, join(grads[1], grads[3])))
        put(0, product(6, grads[3]))
        put_pair((9, 10), product(1, join(packs[0], packs[1])))
        put(11, product(3, packs[1]))
        put(12, product(5, packs[2]))
        put(13, product(7, packs[1]))

    vmem = pl.BlockSpec(memory_space=pltpu.VMEM)
    return pl.pallas_call(
        body,
        in_specs=[pl.BlockSpec(memory_space=pltpu.SMEM)] + [vmem] * 5,
        out_specs=[vmem, vmem],
        out_shape=[
            jax.ShapeDtypeStruct((groups, BLOCKS * 16, LANES), F32),
            jax.ShapeDtypeStruct((groups, BLOCKS * 16, LANES), BF16),
        ],
        scratch_shapes=[
            pltpu.VMEM((rows, 512), BF16),
            pltpu.VMEM((rows, 3 * LANES), BF16),
        ],
        compiler_params=pltpu.CompilerParams(vmem_limit_bytes=24 << 20),
        name="backward",
    )(me, pick, arrived, head_table, cells, hidden)


def pair_sum(keep, other, direct):
    groups, block_rows, _ = keep.shape
    last = block_rows - 16

    def body(keep_ref, other_ref, *out_refs):
        low_lanes = lax.broadcasted_iota(jnp.int32, (16, LANES), 1) < C_OUT
        for g in range(groups):
            out_ref = out_refs[g] if direct else out_refs[0].at[g]
            total = keep_ref[g] + other_ref[g].astype(F32)
            tail = total[last:]
            tail = jnp.where(low_lanes, split_sums(tail[0:8] + tail[8:16]), tail)
            out_ref[0:last, :] = total[0:last].astype(out_ref.dtype)
            out_ref[last:, :] = tail.astype(out_ref.dtype)

    if direct:
        out_shape = [
            jax.ShapeDtypeStruct((block_rows, LANES), BF16 if g else F32) for g in range(groups)
        ]
    else:
        out_shape = [jax.ShapeDtypeStruct((groups, block_rows, LANES), BF16)]
    return pl.pallas_call(
        body,
        out_shape=out_shape,
        compiler_params=pltpu.CompilerParams(vmem_limit_bytes=8 << 20),
        name="pair_sum",
    )(keep, other)


def final_sum(arrived, scale, per_block):
    def body(*refs):
        conv_ref, bias_ref, head_ref = refs[len(arrived) :]
        total = refs[0][...]
        for ref in refs[1 : len(arrived)]:
            total = total + ref[...].astype(F32)
        total = total * scale
        for block, taps in enumerate(HALF_TAPS):
            value = total[block * per_block : (block + 1) * per_block]
            for half, tap in enumerate(taps):
                if tap is not None:
                    conv_ref[tap] = value[:, half * C_OUT : (half + 1) * C_OUT]
        joined = value[0:8] + value[8:16]
        bias_ref[...] = joined[0:1, 0:C_OUT]
        head_ref[...] = joined[1 : 1 + FIELDS, 0:C_OUT]

    return pl.pallas_call(
        body,
        out_shape=[
            jax.ShapeDtypeStruct((TAPS, per_block, C_OUT), F32),
            jax.ShapeDtypeStruct((1, C_OUT), F32),
            jax.ShapeDtypeStruct((FIELDS, C_OUT), F32),
        ],
        compiler_params=pltpu.CompilerParams(vmem_limit_bytes=4 << 20),
        name="final_sum",
    )(*arrived)


def on_device(patches, destination, cotangent, conv_weight, conv_bias, head_weight):
    owners = lax.axis_size("domain")
    my_index = lax.axis_index("domain")
    own_rows = patches.shape[0]
    train_rows = cotangent.shape[0]
    per_pair = (train_rows + owners - 1) // owners
    channels = C_IN // owners
    splits = 16 // channels
    if splits > 1:
        order = np.arange(C_IN).reshape(C_IN // 32, splits, 2, channels)
        order = order.transpose(0, 2, 1, 3).reshape(-1)
        patches = patches[:, :, order]
        conv_weight = conv_weight[order]

    listing = lax.all_to_all(
        spread(destination, owners),
        "domain",
        split_axis=0,
        concat_axis=0,
        tiled=True,
    )
    cells = patches.transpose(1, 0, 2)
    weights = conv_weight.transpose(1, 2, 0)
    slots = owners * per_pair
    bias = conv_bias.reshape(1, C_OUT)
    hidden, pick, head_table = forward_part(
        cells, 0, 4, weights, bias, destination, head_weight.T, slots, per_pair
    )
    me = my_index.astype(jnp.int32).reshape(1)
    rows = cotangent.reshape(train_rows * FIELDS, FINE)
    outgoing = row_copy(listing, me, rows, per_pair)
    arrived = lax.all_to_all(
        outgoing.reshape(owners, per_pair * FIELDS, FINE), "domain", split_axis=0, concat_axis=0, tiled=True
    ).reshape(owners * per_pair * FIELDS, FINE)

    mates = owners // 2
    direct = mates == C_IN // 32
    keep, send = backward(me, pick, arrived, head_table, cells, hidden, direct)
    other = lax.ppermute(send, "domain", [(i, i ^ 1) for i in range(owners)])
    payload = pair_sum(keep, other, direct)

    scale = float((owners * own_rows * PS**3) ** (-0.5))
    if direct:
        arrived = [payload[0]]
        for k in SEND_ORDER:
            arrived.append(lax.ppermute(payload[k], "domain", [(i, i ^ (2 * k)) for i in range(owners)]))
        conv, bias_out, head_out = final_sum(arrived, scale, channels)
        return conv.transpose(1, 0, 2), bias_out.reshape(C_OUT), head_out.T
    groups = [[core_id + 2 * k for k in range(mates)] for core_id in range(2)]
    tail = jnp.repeat(payload[0][:, (BLOCKS - 1) * 16 :], splits, axis=0)
    blocks = payload[0].reshape(C_IN // 32, BLOCKS, splits, channels, LANES)
    blocks = blocks.transpose(0, 2, 1, 3, 4).reshape(mates, BLOCKS * channels, LANES)
    swapped = lax.all_to_all(
        jnp.concatenate([blocks, tail], axis=1),
        "domain",
        split_axis=0,
        concat_axis=0,
        tiled=True,
        axis_index_groups=groups,
    )
    total = jnp.sum(swapped.astype(F32), axis=0) * scale
    tail = total[BLOCKS * channels :, 0:C_OUT]
    tail = tail[0:8] + tail[8:]
    total = total[: BLOCKS * channels].reshape(BLOCKS, channels, 2, C_OUT)
    where = {tap: (b, h) for b, pair in enumerate(HALF_TAPS) for h, tap in enumerate(pair)}
    conv = jnp.stack([total[where[t][0], :, where[t][1]] for t in range(TAPS)], axis=1)
    return conv, tail[0], tail[1 : 1 + FIELDS].T


def solution(mesh):
    placed = (
        P(("groups", "domain"), None, None),
        P(("groups", "domain")),
        P(("groups", "domain"), None, None),
        P(),
        P(),
        P(),
    )
    return jax.shard_map(
        on_device,
        mesh=mesh,
        in_specs=placed,
        out_specs=(P(("groups", "domain"), None, None), P("groups"), P("groups", None)),
        check_vma=False,
    )
```

```python
import jax
import jax.numpy as jnp
import numpy as np
from jax import lax
from jax.experimental import pallas as pl
from jax.experimental.pallas import tpu as pltpu
from jax.sharding import PartitionSpec as P

C_IN = 256
C_OUT = 64
FIELDS = 4
TAPS = 27
PS = 4
PAD = 5
CELLS = PAD**3
FINE = 512
LANES = 128
BLOCKS = 14
SEND_ORDER = (4, 7, 5, 6, 3, 2, 1)
F32 = jnp.float32
BF16 = jnp.bfloat16
HALF_TAPS = [(b * 3 + 1, b * 3 + 2) for b in range(9)]
HALF_TAPS += [(4 * 3, 7 * 3), (5 * 3, 8 * 3), (3 * 3, 6 * 3), (1 * 3, 2 * 3), (None, 0)]


def row_copy(listing, me, rows, per_pair):
    owners, _, own = listing.shape
    lines = owners * per_pair * FIELDS

    def body(me_ref, listing_ref, rows_ref, out_ref):
        hits = (listing_ref[...].reshape(owners, own) == me_ref[0]).astype(F32)
        counts = jnp.broadcast_to(jnp.sum(hits, axis=1, keepdims=True), (owners, LANES)).astype(BF16)
        line = lax.broadcasted_iota(jnp.int32, (lines, owners), 0)
        owner = lax.broadcasted_iota(jnp.int32, (lines, owners), 1)
        before = (owner < line // (per_pair * FIELDS)).astype(F32).astype(BF16)
        starts = jnp.dot(before, counts, preferred_element_type=F32)
        line = lax.broadcasted_iota(jnp.int32, (lines, LANES), 0)
        lane = lax.broadcasted_iota(jnp.int32, (lines, LANES), 1)
        wanted = starts.astype(jnp.int32) * FIELDS + line % (per_pair * FIELDS)
        pick = (wanted == lane).astype(F32).astype(BF16)
        out_ref[...] = jnp.dot(pick, rows_ref[...], preferred_element_type=F32).astype(BF16)

    vmem = pl.BlockSpec(memory_space=pltpu.VMEM)
    return pl.pallas_call(
        body,
        in_specs=[pl.BlockSpec(memory_space=pltpu.SMEM), vmem, vmem],
        out_specs=vmem,
        out_shape=jax.ShapeDtypeStruct((lines, FINE), BF16),
        compiler_params=pltpu.CompilerParams(vmem_limit_bytes=4 << 20),
        cost_estimate=pl.CostEstimate(flops=8 << 30, transcendentals=0, bytes_accessed=1 << 20),
        name="row_copy",
    )(me, listing, rows)


def spread(destination, owners):
    own = destination.shape[0]

    def body(in_ref, out_ref):
        out_ref[...] = jnp.broadcast_to(in_ref[...].reshape(1, 1, own), (owners, 1, own))

    return pl.pallas_call(
        body, out_shape=jax.ShapeDtypeStruct((owners, 1, own), jnp.int32), name="spread"
    )(destination.reshape(1, own))


def turn_terms():
    fine = lax.broadcasted_iota(jnp.int32, (LANES, LANES), 0)
    lane = lax.broadcasted_iota(jnp.int32, (LANES, LANES), 1)
    to = ((fine >> 4) & 3) * 32 + (fine >> 6) * 16 + (fine & 15)
    return (to == lane).astype(F32).astype(BF16)


def head_terms(head):
    rows = jnp.concatenate([jnp.broadcast_to(head[f : f + 1], (32, C_OUT)) for f in range(FIELDS)], axis=0)
    pair = jnp.concatenate([rows, rows], axis=1)
    table = jnp.concatenate([pair] * 4, axis=1)
    row = lax.broadcasted_iota(jnp.int32, table.shape, 0)
    col = lax.broadcasted_iota(jnp.int32, table.shape, 1)
    table = jnp.where((row // 8 % 4) * 2 + row % 2 == col // C_OUT, table, 0.0)
    high = table.astype(BF16)
    return jnp.concatenate([high, (table - high.astype(F32)).astype(BF16)], axis=0)


def forward_part(patches, first, count, weights, bias, destination, head, slots, per_pair):
    own = patches.shape[1]
    rows = 16 * own
    lead = first == 0

    def body(*refs):
        dest_ref, head_ref, x_ref, w_ref, bias_ref = refs[:5]
        hidden_ref = refs[5]
        w2_ref = refs[-1]
        step = pl.program_id(0)

        @pl.when(step == 0)
        def _():
            w2_ref[1, :, 0:C_OUT, :] = jnp.zeros((9, C_OUT, C_IN), BF16)
            for b in range(9):
                w2_ref[0, b] = w_ref[3 * b + 1 : 3 * b + 3].reshape(2 * C_OUT, C_IN)
                w2_ref[1, b, C_OUT:, :] = w_ref[3 * b]
            if lead:
                pick_ref, table_ref = refs[6:8]
                line = lax.broadcasted_iota(jnp.int32, (FIELDS * own, slots * FIELDS), 0)
                lane = lax.broadcasted_iota(jnp.int32, (FIELDS * own, slots * FIELDS), 1)
                wanted = jnp.zeros_like(line)
                for n in range(own):
                    rank = jnp.int32(0)
                    for k in range(n):
                        rank = rank + (dest_ref[k] == dest_ref[n]).astype(jnp.int32)
                    wanted = jnp.where(line % own == n, dest_ref[n] * per_pair + rank, wanted)
                wanted = wanted * FIELDS + line // own
                pick_ref[...] = (wanted == lane).astype(F32).astype(BF16)
                table_ref[...] = head_terms(head_ref[...])

        m1 = step + first
        picked = []
        for shift in range(8):
            s1, s2, s3 = shift // 4, (shift // 2) % 2, shift % 2
            pieces = [
                x_ref[pl.ds((m1 + s1) * 25 + (m2 + s2) * 5 + s3, 4)].reshape(4 * own, C_IN)
                for m2 in range(4)
            ]
            picked.append(jnp.concatenate(pieces, axis=0))
        bias_row = jnp.concatenate([bias_ref[...]] * 4, axis=1)
        for p1 in range(2):
            both = jnp.zeros((rows, 2 * LANES), F32)
            odd = jnp.zeros((rows, LANES), F32)
            for s1 in range(p1 + 1):
                k1 = 1 if p1 == 0 else (2 if s1 == 0 else 0)
                for s3 in range(2):
                    both = both + lax.dot_general(
                        picked[s1 * 4 + s3],
                        w2_ref[s3, k1 * 3 + 1 : k1 * 3 + 3].reshape(2 * LANES, C_IN),
                        (((1,), (1,)), ((), ())),
                        preferred_element_type=F32,
                    )
                    odd = odd + lax.dot_general(
                        picked[s1 * 4 + 2 + s3],
                        w2_ref[s3, k1 * 3],
                        (((1,), (1,)), ((), ())),
                        preferred_element_type=F32,
                    )
            lanes = slice(p1 * 2 * LANES, (p1 + 1) * 2 * LANES)
            total = jnp.concatenate([both[:, :LANES], both[:, LANES:] + odd], axis=1)
            hidden_ref[:, lanes] = total + bias_row

    fixed = lambda *shape: pl.BlockSpec(shape, lambda i: (0,) * len(shape))
    out_specs = [pl.BlockSpec((rows, 512), lambda i: (i, 0))]
    out_shape = [jax.ShapeDtypeStruct((count * rows, 512), F32)]
    if lead:
        out_specs += [fixed(FIELDS * own, slots * FIELDS), fixed(2 * LANES, 512)]
        out_shape += [
            jax.ShapeDtypeStruct((FIELDS * own, slots * FIELDS), BF16),
            jax.ShapeDtypeStruct((2 * LANES, 512), BF16),
        ]
    return pl.pallas_call(
        body,
        grid=(count,),
        in_specs=[
            pl.BlockSpec(memory_space=pltpu.SMEM),
            fixed(FIELDS, C_OUT),
            fixed(CELLS, own, C_IN),
            fixed(TAPS, C_OUT, C_IN),
            fixed(1, C_OUT),
        ],
        out_specs=out_specs,
        out_shape=out_shape,
        scratch_shapes=[pltpu.VMEM((2, 9, LANES, C_IN), BF16)],
        cost_estimate=pl.CostEstimate(
            flops=count * 2 * rows * C_IN * 3600, transcendentals=0, bytes_accessed=4 << 20
        ),
        compiler_params=pltpu.CompilerParams(vmem_limit_bytes=16 << 20),
        name="forward_part",
    )(destination, head, patches, weights, bias)


def split_sums(sums):
    high = sums.astype(BF16).astype(F32)
    return jnp.concatenate([high, sums - high], axis=0)


def backward(me, pick, arrived, head_table, cells, hidden, direct):
    slots = cells.shape[1]
    span = 16 * slots
    rows = 4 * span
    groups = C_IN // 32

    def body(
        me_ref, pick_ref, arrived_ref, head_ref, x_ref, hidden_ref, keep_ref, send_ref, grad_ref, pack_ref
    ):
        lane = lax.broadcasted_iota(jnp.int32, (1, LANES), 1)
        chosen = jnp.dot(pick_ref[...], arrived_ref[...], preferred_element_type=F32).astype(BF16)
        turn = turn_terms()
        turned = [
            jnp.dot(chosen[:, m1 * LANES : (m1 + 1) * LANES], turn, preferred_element_type=F32)
            for m1 in range(4)
        ]
        pieces = []
        for j in range(16):
            piece = jnp.zeros((slots, LANES), F32)
            for f in range(FIELDS):
                part = turned[j // 4][f * slots : (f + 1) * slots]
                shift = (f - j % 4) * 32 % LANES
                part = pltpu.roll(part, shift, 1) if shift else part
                piece = jnp.where(lane // 32 == f, part, piece)
            pieces.append(piece.astype(BF16))
        fields = jnp.concatenate(pieces, axis=0)
        low_lanes = lane < C_OUT
        bias_sum = jnp.zeros((1, 512), F32)
        head_sum = jnp.zeros((LANES, 512), F32)
        for m3 in range(4):
            here = [slice((j * 4 + m3) * slots, (j * 4 + m3 + 1) * slots) for j in range(16)]
            mine = (lane // 2) % 4 == m3
            some = jnp.where(mine, fields, jnp.zeros_like(fields))
            upstream = jnp.dot(
                jnp.concatenate([some, some], axis=1), head_ref[...], preferred_element_type=F32
            )
            hidden = jnp.concatenate([hidden_ref[rows_of, :] for rows_of in here], axis=0)
            gate = jax.nn.sigmoid(hidden)
            active = hidden * gate
            grad = upstream * (gate * (1.0 + hidden * (1.0 - gate)))
            bias_sum = bias_sum + jnp.sum(grad, axis=0, keepdims=True)
            low = grad.astype(BF16)
            for j, rows_of in enumerate(here):
                grad_ref[rows_of, :] = low[j * slots : (j + 1) * slots]
            blk = [grad[:, b * LANES : (b + 1) * LANES] for b in range(4)]
            for k, (lo, hi) in enumerate(((0, 2), (1, 3), (2, 3))):
                packed = jnp.where(low_lanes, pltpu.roll(blk[lo], C_OUT, 1), blk[hi])
                packed = packed.astype(BF16)
                for j, rows_of in enumerate(here):
                    pack_ref[rows_of, k * LANES : (k + 1) * LANES] = packed[j * slots : (j + 1) * slots]
            high = active.astype(BF16)
            for term in (high, (active - high.astype(F32)).astype(BF16)):
                head_sum = head_sum + lax.dot_general(
                    some, term, (((0,), (0,)), ((), ())), preferred_element_type=F32
                )
        row = lax.broadcasted_iota(jnp.int32, (LANES, 512), 0)
        col = lax.broadcasted_iota(jnp.int32, (LANES, 512), 1)
        head_sum = jnp.where((row // 8 % 4) * 2 + row % 2 == col // C_OUT, head_sum, 0.0)
        heads = [
            jnp.sum(head_sum[f * 32 : (f + 1) * 32], axis=0, keepdims=True) for f in range(FIELDS)
        ]
        stacked = jnp.concatenate([bias_sum] + heads + [jnp.zeros((3, 512), F32)], axis=0)
        folded = sum(stacked[:, b * LANES : (b + 1) * LANES] for b in range(4))
        folded = folded + pltpu.roll(folded, C_OUT, 1)
        tail = split_sums(folded)
        first_core = (me_ref[0] & 1) == 0
        home = me_ref[0] >> 1 if direct else 0

        def product(shift, value):
            s1, s2, s3 = shift // 4, (shift // 2) % 2, shift % 2
            pieces = []
            for m in range(16):
                cell = (m // 4 + s1) * 25 + (m % 4 + s2) * 5 + s3
                pieces.append(x_ref[cell : cell + 4].reshape(4 * slots, C_IN))
            return lax.dot_general(
                jnp.concatenate(pieces, axis=0),
                value,
                (((0,), (0,)), ((), ())),
                preferred_element_type=F32,
            )

        def put(block, value):
            split = value.reshape(groups, 2, 16, LANES)
            even, odd = split[:, 0], split[:, 1]
            if block == BLOCKS - 1:
                even, odd = (jnp.where(low_lanes[None], tail[None], half) for half in (even, odd))
            mine = jnp.where(first_core, even, odd)
            other = jnp.where(first_core, odd, even).astype(BF16)
            at = slice(block * 16, (block + 1) * 16)
            for g in range(groups):
                keep_ref[g ^ home, at, :] = mine[g]
                send_ref[g ^ home, at, :] = other[g]

        def put_pair(blocks, value):
            put(blocks[0], value[:, 0:LANES])
            put(blocks[1], value[:, LANES : 2 * LANES])

        grads = [grad_ref[:, b * LANES : (b + 1) * LANES] for b in range(4)]
        packs = [pack_ref[:, b * LANES : (b + 1) * LANES] for b in range(3)]
        join = lambda *parts: jnp.concatenate(parts, axis=1)
        value = product(0, join(*grads))
        put_pair((4, 5), value[:, : 2 * LANES])
        put_pair((7, 8), value[:, 2 * LANES :])
        put_pair((1, 2), product(4, join(grads[2], grads[3])))
        put_pair((3, 6), product(2, join(grads[1], grads[3])))
        put(0, product(6, grads[3]))
        put_pair((9, 10), product(1, join(packs[0], packs[1])))
        put(11, product(3, packs[1]))
        put(12, product(5, packs[2]))
        put(13, product(7, packs[1]))

    vmem = pl.BlockSpec(memory_space=pltpu.VMEM)
    return pl.pallas_call(
        body,
        in_specs=[pl.BlockSpec(memory_space=pltpu.SMEM)] + [vmem] * 5,
        out_specs=[vmem, vmem],
        out_shape=[
            jax.ShapeDtypeStruct((groups, BLOCKS * 16, LANES), F32),
            jax.ShapeDtypeStruct((groups, BLOCKS * 16, LANES), BF16),
        ],
        scratch_shapes=[
            pltpu.VMEM((rows, 512), BF16),
            pltpu.VMEM((rows, 3 * LANES), BF16),
        ],
        compiler_params=pltpu.CompilerParams(vmem_limit_bytes=24 << 20),
        name="backward",
    )(me, pick, arrived, head_table, cells, hidden)


def pair_sum(keep, other, direct):
    groups, block_rows, _ = keep.shape
    last = block_rows - 16

    def body(keep_ref, other_ref, *out_refs):
        low_lanes = lax.broadcasted_iota(jnp.int32, (16, LANES), 1) < C_OUT
        for g in range(groups):
            out_ref = out_refs[g] if direct else out_refs[0].at[g]
            total = keep_ref[g] + other_ref[g].astype(F32)
            tail = total[last:]
            tail = jnp.where(low_lanes, split_sums(tail[0:8] + tail[8:16]), tail)
            out_ref[0:last, :] = total[0:last].astype(out_ref.dtype)
            out_ref[last:, :] = tail.astype(out_ref.dtype)

    if direct:
        out_shape = [
            jax.ShapeDtypeStruct((block_rows, LANES), BF16 if g else F32) for g in range(groups)
        ]
    else:
        out_shape = [jax.ShapeDtypeStruct((groups, block_rows, LANES), BF16)]
    return pl.pallas_call(
        body,
        out_shape=out_shape,
        compiler_params=pltpu.CompilerParams(vmem_limit_bytes=8 << 20),
        name="pair_sum",
    )(keep, other)


def final_sum(arrived, scale, per_block):
    def body(*refs):
        conv_ref, bias_ref, head_ref = refs[len(arrived) :]
        total = refs[0][...]
        for ref in refs[1 : len(arrived)]:
            total = total + ref[...].astype(F32)
        total = total * scale
        for block, taps in enumerate(HALF_TAPS):
            value = total[block * per_block : (block + 1) * per_block]
            for half, tap in enumerate(taps):
                if tap is not None:
                    conv_ref[tap] = value[:, half * C_OUT : (half + 1) * C_OUT]
        joined = value[0:8] + value[8:16]
        bias_ref[...] = joined[0:1, 0:C_OUT]
        head_ref[...] = joined[1 : 1 + FIELDS, 0:C_OUT]

    return pl.pallas_call(
        body,
        out_shape=[
            jax.ShapeDtypeStruct((TAPS, per_block, C_OUT), F32),
            jax.ShapeDtypeStruct((1, C_OUT), F32),
            jax.ShapeDtypeStruct((FIELDS, C_OUT), F32),
        ],
        compiler_params=pltpu.CompilerParams(vmem_limit_bytes=4 << 20),
        name="final_sum",
    )(*arrived)


def on_device(patches, destination, cotangent, conv_weight, conv_bias, head_weight):
    owners = lax.axis_size("domain")
    my_index = lax.axis_index("domain")
    own_rows = patches.shape[0]
    train_rows = cotangent.shape[0]
    per_pair = (train_rows + owners - 1) // owners
    channels = C_IN // owners
    splits = 16 // channels
    if splits > 1:
        order = np.arange(C_IN).reshape(C_IN // 32, splits, 2, channels)
        order = order.transpose(0, 2, 1, 3).reshape(-1)
        patches = patches[:, :, order]
        conv_weight = conv_weight[order]

    listing = lax.all_to_all(
        spread(destination, owners),
        "domain",
        split_axis=0,
        concat_axis=0,
        tiled=True,
    )
    cells = patches.transpose(1, 0, 2)
    weights = conv_weight.transpose(1, 2, 0)
    slots = owners * per_pair
    bias = conv_bias.reshape(1, C_OUT)
    hidden, pick, head_table = forward_part(
        cells, 0, 4, weights, bias, destination, head_weight.T, slots, per_pair
    )
    me = my_index.astype(jnp.int32).reshape(1)
    rows = cotangent.reshape(train_rows * FIELDS, FINE)
    outgoing = row_copy(listing, me, rows, per_pair)
    arrived = lax.all_to_all(
        outgoing.reshape(owners, per_pair * FIELDS, FINE), "domain", split_axis=0, concat_axis=0, tiled=True
    ).reshape(owners * per_pair * FIELDS, FINE)

    mates = owners // 2
    direct = mates == C_IN // 32
    keep, send = backward(me, pick, arrived, head_table, cells, hidden, direct)
    other = lax.ppermute(send, "domain", [(i, i ^ 1) for i in range(owners)])
    payload = pair_sum(keep, other, direct)

    scale = float((owners * own_rows * PS**3) ** (-0.5))
    if direct:
        arrived = [payload[0]]
        for k in SEND_ORDER:
            arrived.append(lax.ppermute(payload[k], "domain", [(i, i ^ (2 * k)) for i in range(owners)]))
        conv, bias_out, head_out = final_sum(arrived, scale, channels)
        return conv.transpose(1, 0, 2), bias_out.reshape(C_OUT), head_out.T
    groups = [[core_id + 2 * k for k in range(mates)] for core_id in range(2)]
    tail = jnp.repeat(payload[0][:, (BLOCKS - 1) * 16 :], splits, axis=0)
    blocks = payload[0].reshape(C_IN // 32, BLOCKS, splits, channels, LANES)
    blocks = blocks.transpose(0, 2, 1, 3, 4).reshape(mates, BLOCKS * channels, LANES)
    swapped = lax.all_to_all(
        jnp.concatenate([blocks, tail], axis=1),
        "domain",
        split_axis=0,
        concat_axis=0,
        tiled=True,
        axis_index_groups=groups,
    )
    total = jnp.sum(swapped.astype(F32), axis=0) * scale
    tail = total[BLOCKS * channels :, 0:C_OUT]
    tail = tail[0:8] + tail[8:]
    total = total[: BLOCKS * channels].reshape(BLOCKS, channels, 2, C_OUT)
    where = {tap: (b, h) for b, pair in enumerate(HALF_TAPS) for h, tap in enumerate(pair)}
    conv = jnp.stack([total[where[t][0], :, where[t][1]] for t in range(TAPS)], axis=1)
    return conv, tail[0], tail[1 : 1 + FIELDS].T


def solution(mesh):
    placed = (
        P(("groups", "domain"), None, None),
        P(("groups", "domain")),
        P(("groups", "domain"), None, None),
        P(),
        P(),
        P(),
    )
    return jax.shard_map(
        on_device,
        mesh=mesh,
        in_specs=placed,
        out_specs=(P(("groups", "domain"), None, None), P("groups"), P("groups", None)),
        check_vma=False,
    )
```
